128 devices in a mesh: seq: 8 (over x, core), tensor: 8 (over z, y_lo), dp: 2 (over y_hi).
Axes of the slice: x: 4, y: 4 (y_hi: 2, y_lo: 2; y = y_hi * 2 + y_lo), z: 4, core: 2. Of those that a mesh axis runs over, the one named last changes fastest.
Arguments:
- ssm_input: bfloat16 [2, 2048, 8192], P('dp', 'seq', 'tensor'), may hold values from -6 to 6
- b_input: bfloat16 [2, 2048, 1024], P('dp', 'seq', 'tensor'), may hold values from -0.125 to 0.125
- c_input: bfloat16 [2, 2048, 1024], P('dp', 'seq', 'tensor'), may hold values from -0.125 to 0.125
- step_size: float32 [2, 128, 2048], P('dp', 'tensor', 'seq'), may hold values from 0 to 2048, as said below
- decay_rate: float32 [128], P('tensor'), may hold values from 0 to 1, as said below
- skip_gain: float32 [128], P('tensor'), may hold values from 0.5 to 2
- resets: int32 [2, 8], P('dp', 'seq'), may hold values 0 or 1
- out_grad: bfloat16 [2, 2048, 4096], P('dp', 'seq'), may hold values from -6 to 6
- out_weight: bfloat16 [4096, 8192], P(('seq', 'dp'), 'tensor'), may hold values from -0.0625 to 0.0625
Outputs:
- grad_input: bfloat16 [2, 2048, 8192], P('dp', 'seq', 'tensor')
- grad_b: float32 [2, 2048, 1024], P('dp', 'seq', 'tensor')
- grad_c: float32 [2, 2048, 1024], P('dp', 'seq', 'tensor')
- grad_weight: float32 [4096, 8192], P(('seq', 'dp'), 'tensor')
The draws below stay inside these ranges and needn't reach their ends.
Inputs may be any that keep to these rules, and one draw needn't show every extreme that they name: `step_size`: positive per-position steps. `decay_rate`: positive per-head rates.
All inputs are finite; a program needn't handle non-finite values. No bound on the sum of `resets` on one device may be relied on, other than what follows from the above.
Results may differ from the reference program's by a relative error of at most 0.017.
Values may be sent and summed in bfloat16 or wider, within the bound.
A program may use at most 128 MiB of HBM per device.

```python
import math
import jax
import jax.numpy as jnp
from jax import lax

D = 4096
P_SIZE = 64
N = 128
HEADS_DEV = 16
Q = 256
GROUPS = 8
HEADS = 128
SEQUENCE_LENGTH = 2048
DIALOGUE_BATCH = 2
NBLOCKS = 8


def draw_decay_rate(key, part):
    pick_key, slow_key, fast_key = jax.random.split(key, 3)
    slow_share = 0.5
    slow_flag = jax.random.uniform(pick_key, (HEADS,)) < slow_share
    slow_rate = jnp.exp(jax.random.uniform(slow_key, (HEADS,), minval=math.log(0.2 / SEQUENCE_LENGTH), maxval=math.log(2.0 / SEQUENCE_LENGTH)))
    fast_rate = jnp.exp(jax.random.uniform(fast_key, (HEADS,), minval=math.log(0.02), maxval=math.log(0.06)))
    return jnp.where(slow_flag, slow_rate, fast_rate).astype(jnp.float32)


def draw_step_size(key, part):
    baseline_key, spike_random_key, amplitude_key = jax.random.split(key, 3)
    baseline_step_count = jax.random.uniform(baseline_key, (DIALOGUE_BATCH, HEADS, SEQUENCE_LENGTH), minval=0.5, maxval=1.5)
    spike_indicator = jax.random.uniform(spike_random_key, (DIALOGUE_BATCH, 1, SEQUENCE_LENGTH)) < 3.0 / SEQUENCE_LENGTH
    spike_magnitude = jax.random.uniform(amplitude_key, (DIALOGUE_BATCH, 1, SEQUENCE_LENGTH), minval=0.2, maxval=0.6) * SEQUENCE_LENGTH
    return jnp.where(spike_indicator, baseline_step_count + spike_magnitude, baseline_step_count).astype(jnp.float32)


def set_ends(result, stream_key, smallest, largest):
    shape = result.shape
    place = [jax.random.randint(jax.random.fold_in(stream_key, axis), (), 0, shape[axis]) for axis in range(len(shape))]
    result = result.at[tuple(place)].set(smallest)
    longest = shape.index(max(shape))
    place[longest] = (place[longest] + 1) % shape[longest]
    return result.at[tuple(place)].set(largest)


def block_scale(key, dims, pieces, smallest, top_value):
    factor_of, own = 1.0, jax.random.fold_in(key, 6)
    for axis_at, parts in pieces:
        heights = jnp.exp(jax.random.uniform(jax.random.fold_in(own, axis_at), (parts,), jnp.float32, smallest / len(pieces), top_value / len(pieces)))
        factor_of = factor_of * jnp.repeat(heights, dims[axis_at] // parts).reshape([-1 if axis == axis_at else 1 for axis in range(len(dims))])
    return factor_of


def noise(own_key, extent, scale, limit, pieces=(), kind=jnp.bfloat16):
    array = scale * jax.random.normal(own_key, extent, jnp.float32)
    if pieces:
        array = array * block_scale(own_key, extent, pieces, -0.22, 0.18)
    return jnp.clip(array, -limit, limit).astype(kind)


def setup_inputs(seed: int = 0) -> dict:
    keys = jax.random.split(jax.random.key(seed), 10)
    return {
        "ssm_input": noise(keys[0], (DIALOGUE_BATCH, SEQUENCE_LENGTH, HEADS * P_SIZE), 1.0, 6.0, ((0, 2), (1, 8), (2, 8))),
        "b_input": noise(keys[1], (DIALOGUE_BATCH, SEQUENCE_LENGTH, GROUPS * N), (N * 16) ** -0.5, 0.125, ((0, 2), (1, 8), (2, 8))),
        "c_input": noise(keys[2], (DIALOGUE_BATCH, SEQUENCE_LENGTH, GROUPS * N), (N * 16) ** -0.5, 0.125, ((0, 2), (1, 8), (2, 8))),
        "step_size": draw_step_size(jax.random.fold_in(keys[9], 71), 0),
        "decay_rate": draw_decay_rate(jax.random.fold_in(keys[9], 71), 0),
        "skip_gain": jnp.clip(jnp.exp(math.log(2.0) - 1.3862944 * jax.random.uniform(keys[5], (HEADS,), jnp.float32) ** block_scale(keys[5], (HEADS,), ((0, 8),), -0.2, 0.2)), 0.5, 2.0),
        "resets": set_ends((jax.random.randint(keys[6], (DIALOGUE_BATCH, NBLOCKS), 0, 8) < 1).astype(jnp.int32), jax.random.fold_in(keys[6], 1), 0, 1),
        "out_grad": noise(keys[7], (DIALOGUE_BATCH, SEQUENCE_LENGTH, D), 1.0, 6.0, ((0, 2), (1, 8))),
        "out_weight": noise(keys[8], (D, HEADS * P_SIZE), (HEADS * P_SIZE) ** -0.5, 0.0625, ((0, 16), (1, 8))),
    }


def contract(pattern, former, latter):
    return jnp.einsum(pattern, former.astype(jnp.float32), latter.astype(jnp.float32))


def block_tables(step_rows, head_rates):
    log_decay = jnp.cumsum(-step_rows * head_rates[..., None], axis=-1)
    last_log = log_decay[..., -1:]
    damping = jnp.exp(last_log[..., 0])
    to_end = jnp.moveaxis(jnp.exp(last_log - log_decay), -1, 0)[..., None]
    from_start = jnp.moveaxis(jnp.exp(log_decay), -1, 0)[..., None]
    positions = jnp.arange(log_decay.shape[-1])
    causal = positions[:, None] >= positions[None, :]
    spread = log_decay[..., :, None] - log_decay[..., None, :]
    weights = jnp.where(causal, jnp.exp(jnp.minimum(spread, 0.0)), 0.0)
    return damping, to_end, from_start, weights


def block_sums(inputs, b_rows, c_rows, grad_rows, to_end, from_start):
    weighted_in = (inputs.astype(jnp.float32) * to_end).astype(jnp.bfloat16)
    weighted_grad = (grad_rows.astype(jnp.float32) * from_start).astype(jnp.bfloat16)
    carried = contract('qgkp,qgn->gkpn', weighted_in, b_rows)
    adjoint = contract('qgkp,qgn->gkpn', weighted_grad, c_rows)
    return carried, adjoint, weighted_in, weighted_grad


def block_grads(inputs, b_rows, c_rows, grad_rows, skip_rows, to_end, from_start, weights, weighted_in, weighted_grad, state_in, adjoint_out):
    scores = contract('ign,jgn->gij', c_rows, b_rows)
    mixing = (weights * scores[:, None]).astype(jnp.bfloat16)
    skip_term = skip_rows[None, :, :, None]
    output = contract('gkij,jgkp->igkp', mixing, inputs) + from_start * contract('gkpn,ign->igkp', state_in, c_rows) + skip_term * inputs.astype(jnp.float32)
    grad_in = contract('gkij,igkp->jgkp', mixing, grad_rows) + to_end * contract('gkpn,jgn->jgkp', adjoint_out, b_rows) + skip_term * grad_rows.astype(jnp.float32)
    products = contract('igkp,jgkp->gkij', grad_rows, inputs)
    paired = (weights * products).astype(jnp.bfloat16)
    grad_b = contract('gkij,ign->jgn', paired, c_rows) + contract('jgkp,gkpn->jgn', weighted_in, adjoint_out)
    grad_c = contract('gkij,jgn->ign', paired, b_rows) + contract('igkp,gkpn->ign', weighted_grad, state_in)
    return output.astype(jnp.bfloat16), grad_in.astype(jnp.bfloat16), grad_b, grad_c


def forward_step(running, sliced):
    kept, carried, damping = sliced
    state_in = kept * running
    return damping[..., None, None] * state_in + carried, state_in


def backward_step(running, sliced):
    kept, adjoint, damping = sliced
    return kept * (damping[..., None, None] * running + adjoint), running


def reference(ssm_input, b_input, c_input, step_size, decay_rate, skip_gain, resets, out_grad, out_weight):
    head_rates = decay_rate.reshape(GROUPS, HEADS_DEV)
    skip_rows = skip_gain.reshape(GROUPS, HEADS_DEV)
    grad_weight = jnp.zeros((D, HEADS * P_SIZE), jnp.float32)
    all_in, all_b, all_c = [], [], []
    for batch_row in range(DIALOGUE_BATCH):
        inputs = ssm_input[batch_row].reshape(NBLOCKS, Q, GROUPS, HEADS_DEV, P_SIZE)
        b_rows = b_input[batch_row].reshape(NBLOCKS, Q, GROUPS, N)
        c_rows = c_input[batch_row].reshape(NBLOCKS, Q, GROUPS, N)
        step_rows = step_size[batch_row].reshape(GROUPS, HEADS_DEV, NBLOCKS, Q).transpose(2, 0, 1, 3)
        incoming = out_grad[batch_row].reshape(NBLOCKS, Q, D)
        keep_rows = (1 - resets[batch_row]).astype(jnp.float32)

        def head_grads(out_rows):
            return jnp.dot(out_rows, out_weight, preferred_element_type=jnp.float32).astype(jnp.bfloat16).reshape(Q, GROUPS, HEADS_DEV, P_SIZE)

        def first_pass(sliced):
            in_rows, brow_block, crow_block, step_block, out_rows = sliced
            damping, to_end, from_start, weights = block_tables(step_block, head_rates)
            carried, adjoint, weighted_in, weighted_grad = block_sums(in_rows, brow_block, crow_block, head_grads(out_rows), to_end, from_start)
            return damping, carried, adjoint

        decays, carried, adjoint = lax.map(first_pass, (inputs, b_rows, c_rows, step_rows, incoming))
        zero_state = jnp.zeros((GROUPS, HEADS_DEV, P_SIZE, N), jnp.float32)
        final_state, states = lax.scan(forward_step, zero_state, (keep_rows, carried, decays))
        final_adjoint, adjoints = lax.scan(backward_step, zero_state, (keep_rows, adjoint, decays), reverse=True)

        def second_pass(accumulated, sliced):
            in_rows, brow_block, crow_block, step_block, out_rows, state_block, adjoint_block = sliced
            grad_rows = head_grads(out_rows)
            damping, to_end, from_start, weights = block_tables(step_block, head_rates)
            carried_now, adjoint_now, weighted_in, weighted_grad = block_sums(in_rows, brow_block, crow_block, grad_rows, to_end, from_start)
            output, grad_in, grad_b, grad_c = block_grads(in_rows, brow_block, crow_block, grad_rows, skip_rows, to_end, from_start, weights, weighted_in, weighted_grad, state_block.astype(jnp.bfloat16), adjoint_block.astype(jnp.bfloat16))
            accumulated = accumulated + jnp.dot(out_rows.T, output.reshape(Q, HEADS * P_SIZE), preferred_element_type=jnp.float32)
            return accumulated, (grad_in, grad_b, grad_c)

        grad_weight, (grad_in, grad_b, grad_c) = lax.scan(second_pass, grad_weight, (inputs, b_rows, c_rows, step_rows, incoming, states, adjoints))
        all_in.append(grad_in.reshape(SEQUENCE_LENGTH, HEADS * P_SIZE))
        all_b.append(grad_b.reshape(SEQUENCE_LENGTH, GROUPS * N))
        all_c.append(grad_c.reshape(SEQUENCE_LENGTH, GROUPS * N))
    return jnp.stack(all_in), jnp.stack(all_b), jnp.stack(all_c), grad_weight
```

```python
import jax
import jax.numpy as jnp
from jax import lax
from jax.experimental import pallas as pl
from jax.experimental.pallas import tpu as pltpu
from jax.sharding import PartitionSpec as P

MESH = pl.DeviceIdType.MESH
BF = jnp.bfloat16
F32 = jnp.float32
Q, HEADS, PS, N = 256, 16, 64, 128
CH, HC, CW = 4, 4, 256
SUB = 2


def mm(a, b, ca=1, cb=0, precision=None):
    return lax.dot_general(
        a, b, (((ca,), (cb,)), ((), ())), preferred_element_type=F32, precision=precision
    )


def kernel(
    x_ref, b_ref, c_ref, step_ref, rate_ref, skip_ref, reset_ref, og_ref, w_ref,
    gin_ref, gb_ref, gc_ref, gw_ref,
    wb, oga, ogs, ogt, xm, mix, wt, ee, te, win, wg, car, fin, fout, stt,
    yi, outs, hp, hs, hr, gg, adl, ain, aout, adt, gi,
    ds, dr, dx, dxr, rowbuf, colbuf, psum,
    loc_sem, ogl_sem, w_send, w_recv, wc_send, wc_recv, oy_send, oy_recv, oz_send, oz_recv,
    f_send, f_recv, a_send, a_recv, o_send, o_recv, h_send, h_recv,
    dc_send, dc_recv, dx_send, dx_recv,
):
    s, t, d = lax.axis_index("seq"), lax.axis_index("tensor"), lax.axis_index("dp")
    x, core = s // 2, lax.rem(s, 2)
    z, yl = t // 2, lax.rem(t, 2)

    def xdev(r):
        return (lax.rem(x + r, 4) * 2 + core, t, d)

    def zdev(r):
        return (s, lax.rem(z + r, 4) * 2 + yl, d)

    twin = (x * 2 + 1 - core, t, d)
    partner = (s, t, 1 - d)
    nxt = (lax.rem(s + 1, 8), t, d)
    prv = (lax.rem(s + 7, 8), t, d)

    bar = pltpu.get_barrier_semaphore()
    peers = [xdev(1), xdev(2), xdev(3), zdev(1), zdev(2), zdev(3), twin, partner, nxt, prv]
    for p in peers:
        pl.semaphore_signal(bar, inc=1, device_id=p, device_id_type=MESH)
    pl.semaphore_wait(bar, len(peers))

    def remote(src, dst, ssem, rsem, dev):
        return pltpu.make_async_remote_copy(
            src_ref=src, dst_ref=dst, send_sem=ssem, recv_sem=rsem, device_id=dev, device_id_type=MESH
        )

    def cols(c):
        return pl.ds(c * CW, CW)

    ogl = []
    for k in range(8):
        cp = pltpu.make_async_copy(
            og_ref.at[pl.ds(z * 64, 64), pl.ds((2 * k + 1 - d) * 256, 256)],
            ogs.at[:, pl.ds(k * 256, 256)], ogl_sem.at[0, k])
        cp.start()
        ogl.append(cp)
    wsends = []
    for c in range(CH):
        for r in (1, 3, 2):
            cp = remote(w_ref.at[:, cols(c)], wb.at[c, s], w_send.at[c, r - 1], w_recv.at[c, r - 1], xdev(r))
            cp.start()
            wsends.append(cp)
        cp = remote(w_ref.at[:, cols(c)], wb.at[c, s], wc_send.at[c, 0], wc_recv.at[c, 0], twin)
        cp.start()
        wsends.append(cp)
    for cp in ogl:
        cp.wait()
    RS = 64 // SUB

    def ogrows(zz, u):
        return pl.ds(Q + zz * 64 + u * RS, RS)

    oysends = []
    for u in range(SUB):
        cp = remote(ogs.at[pl.ds(u * RS, RS), :], oga.at[ogrows(z, u), :], oy_send.at[u], oy_recv.at[u], partner)
        cp.start()
        oysends.append(cp)
    locs = []
    for c in range(CH):
        cp = pltpu.make_async_copy(w_ref.at[:, cols(c)], wb.at[c, s], loc_sem.at[c])
        cp.start()
        locs.append(cp)
    for k in range(8):
        cp = pltpu.make_async_copy(
            og_ref.at[:, pl.ds((2 * k + d) * 256, 256)], oga.at[pl.ds(0, Q), pl.ds(k * 256, 256)], ogl_sem.at[1, k])
        cp.start()
        locs.append(cp)

    rate = rate_ref[...]
    eye = lax.broadcasted_iota(jnp.int32, (HEADS, HEADS), 0) == lax.broadcasted_iota(jnp.int32, (HEADS, HEADS), 1)
    rate_col = jnp.sum(jnp.where(eye, jnp.broadcast_to(rate, (HEADS, HEADS)), 0.0), axis=1, keepdims=True)
    run = -step_ref[...] * rate_col
    lane = lax.broadcasted_iota(jnp.int32, (HEADS, Q), 1)
    for k in range(8):
        run = run + jnp.where(lane >= (1 << k), pltpu.roll(run, 1 << k, 1), 0.0)
    rowbuf[...] = jnp.zeros_like(rowbuf)
    rowbuf[0:HEADS, :] = run
    lcol = jnp.transpose(rowbuf[...])
    colbuf[...] = lcol
    hrow = lax.broadcasted_iota(jnp.int32, (128, HEADS * PS), 0)
    hcol = lax.broadcasted_iota(jnp.int32, (128, HEADS * PS), 1) // PS
    spread = jnp.where(hrow == hcol, 1.0, 0.0).astype(F32)
    hi = lax.Precision.HIGHEST
    ee[...] = mm(jnp.exp(lcol), spread, precision=hi)
    te[...] = mm(jnp.exp(lcol[Q - 1 : Q, :] - lcol), spread, precision=hi)
    skip_row = mm(jnp.broadcast_to(skip_ref[...], (8, HEADS)), spread[0:HEADS, :], precision=hi)[0:1, :]
    keep = (1 - reset_ref[0, 0]).astype(F32)

    bm, cm = b_ref[...], c_ref[...]
    win[...] = (x_ref[...].astype(F32) * te[...]).astype(BF)
    car[...] = mm(bm, win[...], 0, 0)

    def decay(c):
        return ee[Q - 1 : Q, cols(c)]

    def forward_step(c):
        @pl.when(s == 0)
        def _():
            stt[c] = jnp.zeros((N, CW), BF)
            fout[c] = car[:, cols(c)]

        @pl.when(s > 0)
        def _():
            remote(fout.at[c], fin.at[c], f_send.at[c], f_recv.at[c], nxt).wait_recv()
            state = keep * fin[c]
            stt[c] = state.astype(BF)
            fout[c] = decay(c) * state + car[:, cols(c)]

        @pl.when(s < 7)
        def _():
            remote(fout.at[c], fin.at[c], f_send.at[c], f_recv.at[c], nxt).start()

    scores = mm(cm, bm, 1, 1)
    ii = lax.broadcasted_iota(jnp.int32, (Q, Q), 0)
    jj = lax.broadcasted_iota(jnp.int32, (Q, Q), 1)
    causal = ii >= jj
    mlane = lax.broadcasted_iota(jnp.int32, (1, CW), 1) // PS
    masks = [jnp.where(mlane == k, 1.0, 0.0).astype(BF) for k in range(HC)]

    def intra(c):
        xc = x_ref[:, cols(c)]
        for k in range(HC):
            h = c * HC + k
            gap = colbuf[:, h : h + 1] - rowbuf[h : h + 1, :]
            w = jnp.where(causal, jnp.exp(jnp.minimum(gap, 0.0)), 0.0)
            wt[h] = w
            mix[h] = (w * scores).astype(BF)
            xm[c, k * Q : (k + 1) * Q, :] = xc * masks[k]
        acc = skip_row[:, c * CW : (c + 1) * CW] * xc.astype(F32)
        for k in range(HC):
            acc = acc + mm(mix[c * HC + k], xm[c, k * Q : (k + 1) * Q, :])
        yi[:, cols(c)] = acc

    ozsends = []

    def share_og(u):
        remote(ogs.at[pl.ds(u * RS, RS), :], oga.at[ogrows(z, u), :], oy_send.at[u], oy_recv.at[u], partner).wait_recv()
        for r in (1, 3, 2):
            piece = oga.at[ogrows(z, u), :]
            cp = remote(piece, piece, oz_send.at[r - 1, u], oz_recv.at[r - 1, u], zdev(r))
            cp.start()
            ozsends.append(cp)

    intra(0)
    intra(1)
    share_og(0)
    intra(2)
    share_og(1)
    intra(3)

    osends = []

    def output(c):
        o = yi[:, cols(c)] + ee[:, cols(c)] * mm(cm, stt[c])
        outs[c, 0:Q, :] = o.astype(BF)
        cp = remote(outs.at[c, pl.ds(0, Q), :], outs.at[c, pl.ds(Q, Q), :], o_send.at[c], o_recv.at[c], partner)
        cp.start()
        osends.append(cp)

    fsends = []

    def share_w(c):
        for r in (1, 3, 2):
            frm = lax.rem(x + 4 - r, 4) * 2 + core
            remote(w_ref.at[:, cols(c)], wb.at[c, frm], w_send.at[c, r - 1], w_recv.at[c, r - 1], xdev(r)).wait_recv()
            cp = remote(wb.at[c, frm], wb.at[c, frm], wc_send.at[c, r], wc_recv.at[c, r], twin)
            cp.start()
            fsends.append(cp)

    hsends = []

    def head(c):
        for r in range(4):
            frm = lax.rem(x + 4 - r, 4) * 2 + 1 - core
            remote(wb.at[c, frm], wb.at[c, frm], wc_send.at[c, r], wc_recv.at[c, r], twin).wait_recv()
        wmat = wb[c].reshape(8 * 256, CW)
        hs[c] = mm(oga[Q : 2 * Q, :], wmat).astype(BF)
        cp = remote(hs.at[c], hr.at[c], h_send.at[c], h_recv.at[c], partner)
        cp.start()
        hsends.append(cp)
        hp[c] = mm(oga[0:Q, :], wmat)

    def head_grad(c):
        remote(hs.at[c], hr.at[c], h_send.at[c], h_recv.at[c], partner).wait_recv()
        g = (hp[c] + hr[c].astype(F32)).astype(BF)
        gg[:, cols(c)] = g
        wgc = (g.astype(F32) * ee[:, cols(c)]).astype(BF)
        wg[:, cols(c)] = wgc
        adl[c] = mm(cm, wgc, 0, 0)

    def backward_step(c):
        @pl.when(s == 7)
        def _():
            adt[c] = jnp.zeros((N, CW), BF)
            aout[c] = keep * adl[c]

        @pl.when(s < 7)
        def _():
            remote(aout.at[c], ain.at[c], a_send.at[c], a_recv.at[c], prv).wait_recv()
            back = ain[c]
            adt[c] = back.astype(BF)
            aout[c] = keep * (decay(c) * back + adl[c])

        @pl.when(s > 0)
        def _():
            remote(aout.at[c], ain.at[c], a_send.at[c], a_recv.at[c], prv).start()

    def within_grads(c):
        gc = gg[:, cols(c)]
        prod = mm(gc, xm[c], 1, 1)
        acc = skip_row[:, c * CW : (c + 1) * CW] * gc.astype(F32)
        tot = None
        for k in range(HC):
            h = c * HC + k
            paired = (wt[h] * prod[:, k * Q : (k + 1) * Q]).astype(BF).astype(F32)
            tot = paired if tot is None else tot + paired
            acc = acc + mm(mix[h], gc * masks[k], 0, 0)
        psum[...] = tot if c == 0 else psum[...] + tot
        gi[:, cols(c)] = acc

    def finish(c):
        gin_ref[:, cols(c)] = (gi[:, cols(c)] + te[:, cols(c)] * mm(bm, adt[c])).astype(BF)
        nb = mm(win[:, cols(c)], adt[c], 1, 1)
        nc = mm(wg[:, cols(c)], stt[c], 1, 1)
        gb_ref[...] = nb if c == 0 else gb_ref[...] + nb
        gc_ref[...] = nc if c == 0 else gc_ref[...] + nc

    dcsends, dxsends = [], []

    def weight_partial(c):
        remote(outs.at[c, pl.ds(0, Q), :], outs.at[c, pl.ds(Q, Q), :], o_send.at[c], o_recv.at[c], partner).wait_recv()
        oc = outs[c]
        for r in (2, 1, 3, 0):
            other = lax.rem(x + r, 4) * 2 + 1 - core
            ds[c, r] = mm(ogt[other], oc).astype(BF)
            cp = remote(ds.at[c, r], dr.at[c, r], dc_send.at[c, r], dc_recv.at[c, r], twin)
            cp.start()
            dcsends.append(cp)

    def weight_send(c):
        oc = outs[c]
        for r in (2, 1, 3, 0):
            own = mm(ogt[lax.rem(x + r, 4) * 2 + core], oc)
            remote(ds.at[c, r], dr.at[c, r], dc_send.at[c, r], dc_recv.at[c, r], twin).wait_recv()
            both = own + dr[c, r].astype(F32)
            if r == 0:
                gw_ref[:, cols(c)] = both
            else:
                dx[c, r - 1] = both.astype(BF)
                cp = remote(dx.at[c, r - 1], dxr.at[c, r - 1], dx_send.at[c, r - 1], dx_recv.at[c, r - 1], xdev(r))
                cp.start()
                dxsends.append(cp)

    def weight_sum(c):
        tot = gw_ref[:, cols(c)]
        for r in range(1, 4):
            remote(dx.at[c, r - 1], dxr.at[c, r - 1], dx_send.at[c, r - 1], dx_recv.at[c, r - 1], xdev(r)).wait_recv()
            tot = tot + dxr[c, r - 1].astype(F32)
        gw_ref[:, cols(c)] = tot

    for c in range(CH):
        forward_step(c)
        output(c)
    for cp in locs:
        cp.wait()
    share_w(0)
    for r in (1, 2, 3):
        frm = lax.rem(z + 4 - r, 4)
        for u in range(SUB):
            piece = oga.at[ogrows(frm, u), :]
            remote(piece, piece, oz_send.at[r - 1, u], oz_recv.at[r - 1, u], zdev(r)).wait_recv()
    for k in range(8):
        ogt[k] = jnp.transpose(oga[:, k * 256 : (k + 1) * 256])
    head(0)
    share_w(1)
    head(1)
    weight_partial(0)
    share_w(2)
    head(2)
    weight_send(0)
    weight_partial(1)
    share_w(3)
    head(3)
    head_grad(0)
    weight_send(1)
    backward_step(0)
    head_grad(1)
    weight_partial(2)
    backward_step(1)
    head_grad(2)
    weight_send(2)
    backward_step(2)
    weight_partial(3)
    head_grad(3)
    weight_send(3)
    backward_step(3)
    for c in range(CH):
        within_grads(c)
        finish(c)
    pb = psum[...].astype(BF)
    gb_ref[...] = gb_ref[...] + mm(pb, cm, 0, 0)
    gc_ref[...] = gc_ref[...] + mm(pb, bm)
    for c in range(CH):
        weight_sum(c)

    for cp in wsends + oysends + ozsends + fsends + osends + hsends + dcsends + dxsends:
        cp.wait_send()
    for c in range(CH):

        @pl.when(s < 7)
        def _():
            remote(fout.at[c], fin.at[c], f_send.at[c], f_recv.at[c], nxt).wait_send()

        @pl.when(s > 0)
        def _():
            remote(aout.at[c], ain.at[c], a_send.at[c], a_recv.at[c], prv).wait_send()


def body(ssm_input, b_input, c_input, step_size, decay_rate, skip_gain, resets, out_grad, out_weight):
    vm, anym = pl.BlockSpec(memory_space=pltpu.VMEM), pl.BlockSpec(memory_space=pl.ANY)
    width = HEADS * PS
    dma = pltpu.SemaphoreType.DMA
    v = pltpu.VMEM
    scratch = [
        v((CH, 8, 256, CW), BF), v((2 * Q, 2048), BF), v((64, 2048), BF), v((8, 256, 2 * Q), BF),
        v((CH, HC * Q, CW), BF), v((HEADS, Q, Q), BF), v((HEADS, Q, Q), F32),
        v((Q, width), F32), v((Q, width), F32), v((Q, width), BF), v((Q, width), BF),
        v((N, width), F32), v((CH, N, CW), F32), v((CH, N, CW), F32), v((CH, N, CW), BF),
        v((Q, width), F32), v((CH, 2 * Q, CW), BF), v((CH, Q, CW), F32), v((CH, Q, CW), BF), v((CH, Q, CW), BF),
        v((Q, width), BF), v((CH, N, CW), F32), v((CH, N, CW), F32), v((CH, N, CW), F32), v((CH, N, CW), BF),
        v((Q, width), F32),
        v((CH, 4, 256, CW), BF), v((CH, 4, 256, CW), BF), v((CH, 3, 256, CW), BF), v((CH, 3, 256, CW), BF),
        v((128, Q), F32), v((Q, 128), F32), v((Q, Q), F32),
        dma((CH,)), dma((2, 8)), dma((CH, 3)), dma((CH, 3)), dma((CH, 4)), dma((CH, 4)), dma((SUB,)), dma((SUB,)),
        dma((3, SUB)), dma((3, SUB)),
        dma((CH,)), dma((CH,)), dma((CH,)), dma((CH,)), dma((CH,)), dma((CH,)), dma((CH,)), dma((CH,)),
        dma((CH, 4)), dma((CH, 4)), dma((CH, 3)), dma((CH, 3)),
    ]
    gin, gb, gc, gw = pl.pallas_call(
        kernel,
        out_shape=(
            jax.ShapeDtypeStruct((Q, width), BF),
            jax.ShapeDtypeStruct((Q, N), F32),
            jax.ShapeDtypeStruct((Q, N), F32),
            jax.ShapeDtypeStruct((256, width), F32),
        ),
        in_specs=[vm, vm, vm, vm, vm, vm, pl.BlockSpec(memory_space=pltpu.SMEM), anym, anym],
        out_specs=(vm, vm, vm, vm),
        scratch_shapes=scratch,
        compiler_params=pltpu.CompilerParams(
            collective_id=0, has_side_effects=True, vmem_limit_bytes=60 * 2**20
        ),
        name="block_backward",
    )(
        ssm_input[0], b_input[0], c_input[0], step_size[0], decay_rate.reshape(1, HEADS),
        skip_gain.reshape(1, HEADS), resets, out_grad[0], out_weight,
    )
    return gin[None], gb[None], gc[None], gw


def solution(mesh):
    in_specs = (
        P("dp", "seq", "tensor"),
        P("dp", "seq", "tensor"),
        P("dp", "seq", "tensor"),
        P("dp", "tensor", "seq"),
        P("tensor"),
        P("tensor"),
        P("dp", "seq"),
        P("dp", "seq", None),
        P(("seq", "dp"), "tensor"),
    )
    out_specs = (
        P("dp", "seq", "tensor"),
        P("dp", "seq", "tensor"),
        P("dp", "seq", "tensor"),
        P(("seq", "dp"), "tensor"),
    )
    return jax.shard_map(body, mesh=mesh, in_specs=in_specs, out_specs=out_specs, check_vma=False)
```

```python
import jax
import jax.numpy as jnp
from jax import lax
from jax.experimental import pallas as pl
from jax.experimental.pallas import tpu as pltpu
from jax.sharding import PartitionSpec as P

MESH = pl.DeviceIdType.MESH
BF = jnp.bfloat16
F32 = jnp.float32
Q, HEADS, PS, N = 256, 16, 64, 128
CH, HC, CW = 4, 4, 256
SUB = 2


def mm(a, b, ca=1, cb=0, precision=None):
    return lax.dot_general(
        a, b, (((ca,), (cb,)), ((), ())), preferred_element_type=F32, precision=precision
    )


def kernel(
    x_ref, b_ref, c_ref, step_ref, rate_ref, skip_ref, reset_ref, og_ref, w_ref,
    gin_ref, gb_ref, gc_ref, gw_ref,
    wb, oga, ogs, ogt, xm, mix, wt, ee, te, win, wg, stt, adt, yi, outs, hp, hs, hr, gg, gi,
    cx, cxr, fb, fbr, sacc, sx, al, alr, ab, abr, ax,
    ds, dr, da, dar, dk, db, dbr, rowbuf, colbuf, psum,
    loc_sem, ogl_sem, w_send, w_recv, wr_send, wr_recv, wc_send, wc_recv, oy_send, oy_recv, oz_send, oz_recv,
    cx_send, cx_recv, f_send, f_recv, sx_send, sx_recv, al_send, al_recv, a_send, a_recv, ax_send, ax_recv,
    o_send, o_recv, h_send, h_recv, dc_send, dc_recv, da_send, da_recv, db_send, db_recv,
):
    s, t, d = lax.axis_index("seq"), lax.axis_index("tensor"), lax.axis_index("dp")
    x, core = s // 2, lax.rem(s, 2)
    z, yl = t // 2, lax.rem(t, 2)

    def xdev(r):
        return (lax.rem(x + r, 4) * 2 + core, t, d)

    def zdev(r):
        return (s, lax.rem(z + r, 4) * 2 + yl, d)

    twin = (x * 2 + 1 - core, t, d)
    partner = (s, t, 1 - d)

    bar = pltpu.get_barrier_semaphore()
    peers = [xdev(1), xdev(2), xdev(3), zdev(1), zdev(2), zdev(3), twin, partner]
    for p in peers:
        pl.semaphore_signal(bar, inc=1, device_id=p, device_id_type=MESH)
    pl.semaphore_wait(bar, len(peers))

    def remote(src, dst, ssem, rsem, dev):
        return pltpu.make_async_remote_copy(
            src_ref=src, dst_ref=dst, send_sem=ssem, recv_sem=rsem, device_id=dev, device_id_type=MESH
        )

    def cols(c):
        return pl.ds(c * CW, CW)

    ogl = []
    for k in range(8):
        cp = pltpu.make_async_copy(
            og_ref.at[pl.ds(z * 64, 64), pl.ds((2 * k + 1 - d) * 256, 256)],
            ogs.at[:, pl.ds(k * 256, 256)], ogl_sem.at[0, k])
        cp.start()
        ogl.append(cp)
    wsends = []

    def w_copy(c, r):
        k = 0 if r == 1 else 1
        return remote(w_ref.at[:, cols(c)], wb.at[c, s], w_send.at[c, k], w_recv.at[c, k], xdev(r))

    def w_twin(c, j, frm):
        return remote(wb.at[c, frm], wb.at[c, frm], wc_send.at[c, j], wc_recv.at[c, j], twin)

    def send_w(c):
        own = remote(w_ref.at[:, cols(c)], wb.at[c, s], wc_send.at[c, 0], wc_recv.at[c, 0], twin)
        for cp in (w_copy(c, 1), w_copy(c, 3), own):
            cp.start()
            wsends.append(cp)

    for cp in ogl:
        cp.wait()
    RS = 64 // SUB

    def ogrows(zz, u):
        return pl.ds(Q + zz * 64 + u * RS, RS)

    oysends = []
    for u in range(SUB):
        cp = remote(ogs.at[pl.ds(u * RS, RS), :], oga.at[ogrows(z, u), :], oy_send.at[u], oy_recv.at[u], partner)
        cp.start()
        oysends.append(cp)
    send_w(0)
    send_w(1)
    locs = []
    for c in range(CH):
        cp = pltpu.make_async_copy(w_ref.at[:, cols(c)], wb.at[c, s], loc_sem.at[c])
        cp.start()
        locs.append(cp)
    for k in range(8):
        cp = pltpu.make_async_copy(
            og_ref.at[:, pl.ds((2 * k + d) * 256, 256)], oga.at[pl.ds(0, Q), pl.ds(k * 256, 256)], ogl_sem.at[1, k])
        cp.start()
        locs.append(cp)

    rate = rate_ref[...]
    eye = lax.broadcasted_iota(jnp.int32, (HEADS, HEADS), 0) == lax.broadcasted_iota(jnp.int32, (HEADS, HEADS), 1)
    rate_col = jnp.sum(jnp.where(eye, jnp.broadcast_to(rate, (HEADS, HEADS)), 0.0), axis=1, keepdims=True)
    run = -step_ref[...] * rate_col
    lane = lax.broadcasted_iota(jnp.int32, (HEADS, Q), 1)
    for k in range(8):
        run = run + jnp.where(lane >= (1 << k), pltpu.roll(run, 1 << k, 1), 0.0)
    rowbuf[...] = jnp.zeros_like(rowbuf)
    rowbuf[0:HEADS, :] = run
    lcol = jnp.transpose(rowbuf[...])
    colbuf[...] = lcol
    hrow = lax.broadcasted_iota(jnp.int32, (128, HEADS * PS), 0)
    hcol = lax.broadcasted_iota(jnp.int32, (128, HEADS * PS), 1) // PS
    spread = jnp.where(hrow == hcol, 1.0, 0.0).astype(F32)
    hi = lax.Precision.HIGHEST
    ee[...] = mm(jnp.exp(lcol), spread, precision=hi)
    te[...] = mm(jnp.exp(lcol[Q - 1 : Q, :] - lcol), spread, precision=hi)
    skip_row = mm(jnp.broadcast_to(skip_ref[...], (8, HEADS)), spread[0:HEADS, :], precision=hi)[0:1, :]
    keep = (1 - reset_ref[0, 0]).astype(F32)

    bm, cm = b_ref[...], c_ref[...]
    win[...] = (x_ref[...].astype(F32) * te[...]).astype(BF)
    HW = CW // 2
    halves = [[slice(c * CW + k * HW, c * CW + (k + 1) * HW) for c in range(CH)] for k in range(2)]
    my_half = pl.ds(pl.multiple_of(core * HW, HW), HW)
    row8 = lax.broadcasted_iota(jnp.int32, (8, HW), 0)
    row16 = lax.broadcasted_iota(jnp.int32, (16, HW), 0)
    for c in range(CH):
        part = mm(bm, win[:, cols(c)], 0, 0)
        for k in range(2):
            cx[k, c, 0:N, :] = part[:, k * HW : (k + 1) * HW]
            gain = jnp.broadcast_to(ee[Q - 1 : Q, halves[k][c]], (8, HW))
            cx[k, c, N : N + 8, :] = jnp.where(row8 == 0, gain, keep)

    def first(a, b):
        return jnp.where(core == 0, a, b), jnp.where(core == 0, b, a)

    def gains(c):
        mine, its = cx[core, c, N : N + 8, :], cxr[c, N : N + 8, :]
        (d0, d1), (k0, k1) = first(mine[0:1], its[0:1]), first(mine[1:2], its[1:2])
        return d0, d1, k0, k1

    def message(ref, c, carry, gain):
        up = gain.astype(BF).astype(F32)
        ref[c, 0:N, :] = carry.astype(BF)
        ref[c, N : N + 16, :] = jnp.where(row16 == 0, up, jnp.where(row16 == 1, gain - up, 0.0)).astype(BF)

    def extend(ref, r, c, total):
        g = ref[r - 1, c, N : N + 16, :].astype(F32)
        return (g[0:1] + g[1:2]) * total + ref[r - 1, c, 0:N, :].astype(F32)

    cx_copy = remote(cx.at[1 - core], cxr, cx_send.at[0], cx_recv.at[0], twin)
    sx_copy = remote(sx, stt.at[:, :, my_half], sx_send.at[0], sx_recv.at[0], twin)

    def f_copy(r):
        return remote(fb, fbr.at[r - 1], f_send.at[r - 1], f_recv.at[r - 1], xdev(r))

    def states_send():
        cx_copy.wait_recv()
        for c in range(CH):
            d0, d1, k0, k1 = gains(c)
            c0, c1 = first(cx[core, c, 0:N, :], cxr[c, 0:N, :])
            message(fb, c, d1 * k1 * c0 + c1, d1 * k1 * d0 * k0)
        for r in (1, 2, 3):

            @pl.when(x + r < 4)
            def _():
                f_copy(r).start()

    def states_done():
        sacc[...] = jnp.zeros_like(sacc)
        for r in (3, 2, 1):

            @pl.when(x >= r)
            def _():
                f_copy(r).wait_recv()
                for c in range(CH):
                    sacc[c] = extend(fbr, r, c, sacc[c])

        for c in range(CH):
            d0, d1, k0, k1 = gains(c)
            c0, c1 = first(cx[core, c, 0:N, :], cxr[c, 0:N, :])
            st0 = k0 * sacc[c]
            st1 = k1 * (d0 * st0 + c0)
            mine, its = first(st0, st1)
            stt[c, :, my_half] = mine.astype(BF)
            sx[c] = its.astype(BF)
        sx_copy.start()

    def al_copy(c):
        return remote(al.at[c, 1 - core], alr.at[c], al_send.at[c], al_recv.at[c], twin)

    def a_copy(c, r):
        return remote(ab.at[c], abr.at[r - 1, c], a_send.at[c, r - 1], a_recv.at[c, r - 1], xdev(4 - r))

    def ax_copy(c):
        return remote(ax.at[c], adt.at[c, :, my_half], ax_send.at[c], ax_recv.at[c], twin)

    def adjoint_send(c):
        al_copy(c).wait_recv()
        d0, d1, k0, k1 = gains(c)
        a0, a1 = first(al[c, core], alr[c])
        message(ab, c, k0 * (d0 * k1 * a1 + a0), d1 * k1 * d0 * k0)
        for r in (1, 2, 3):

            @pl.when(x >= r)
            def _():
                a_copy(c, r).start()

    def adjoint_done(c):
        sacc[c] = jnp.zeros((N, HW), F32)
        for r in (3, 2, 1):

            @pl.when(x + r < 4)
            def _():
                a_copy(c, r).wait_recv()
                sacc[c] = extend(abr, r, c, sacc[c])

        d0, d1, k0, k1 = gains(c)
        a0, a1 = first(al[c, core], alr[c])
        ad1 = sacc[c]
        mine, its = first(k1 * (d1 * ad1 + a1), ad1)
        adt[c, :, my_half] = mine.astype(BF)
        ax[c] = its.astype(BF)
        ax_copy(c).start()

    scores = mm(cm, bm, 1, 1)
    ii = lax.broadcasted_iota(jnp.int32, (Q, Q), 0)
    jj = lax.broadcasted_iota(jnp.int32, (Q, Q), 1)
    causal = ii >= jj
    mlane = lax.broadcasted_iota(jnp.int32, (1, CW), 1) // PS
    masks = [jnp.where(mlane == k, 1.0, 0.0).astype(BF) for k in range(HC)]

    def intra(c):
        xc = x_ref[:, cols(c)]
        for k in range(HC):
            h = c * HC + k
            gap = colbuf[:, h : h + 1] - rowbuf[h : h + 1, :]
            w = jnp.where(causal, jnp.exp(jnp.minimum(gap, 0.0)), 0.0)
            wt[h] = w
            mix[h] = (w * scores).astype(BF)
            xm[c, k * Q : (k + 1) * Q, :] = xc * masks[k]
        acc = skip_row[:, c * CW : (c + 1) * CW] * xc.astype(F32)
        for k in range(HC):
            acc = acc + mm(mix[c * HC + k], xm[c, k * Q : (k + 1) * Q, :])
        yi[:, cols(c)] = acc

    ozsends = []

    def share_og(u):
        remote(ogs.at[pl.ds(u * RS, RS), :], oga.at[ogrows(z, u), :], oy_send.at[u], oy_recv.at[u], partner).wait_recv()
        for r in (1, 3, 2):
            piece = oga.at[ogrows(z, u), :]
            cp = remote(piece, piece, oz_send.at[r - 1, u], oz_recv.at[r - 1, u], zdev(r))
            cp.start()
            ozsends.append(cp)


    osends = []

    def output(c):
        o = yi[:, cols(c)] + ee[:, cols(c)] * mm(cm, stt[c])
        outs[c, 0:Q, :] = o.astype(BF)
        cp = remote(outs.at[c, pl.ds(0, Q), :], outs.at[c, pl.ds(Q, Q), :], o_send.at[c], o_recv.at[c], partner)
        cp.start()
        osends.append(cp)

    fsends = []
    HR = 128

    def chip(r):
        return lax.rem(x + r, 4)

    def wr_copy(c, k):
        rows = pl.ds(k * HR, HR)
        piece = wb.at[c, chip(3 if k == 0 else 1) * 2 + core, rows]
        return remote(piece, piece, wr_send.at[c, k], wr_recv.at[c, k], xdev(1 if k == 0 else 3))

    def relay_w(c):
        for k, r in ((0, 1), (1, 3)):
            w_copy(c, r).wait_recv()
            cp = wr_copy(c, k)
            cp.start()
            fsends.append(cp)
            cp = w_twin(c, 1 + k, chip(3 if k == 0 else 1) * 2 + core)
            cp.start()
            fsends.append(cp)

    def share_w(c):
        for k in range(2):
            wr_copy(c, k).wait_recv()
        cp = w_twin(c, 3, chip(2) * 2 + core)
        cp.start()
        fsends.append(cp)

    hsends = []

    def head(c):
        for j, r in enumerate((0, 3, 1, 2)):
            w_twin(c, j, chip(r) * 2 + 1 - core).wait_recv()
        wmat = wb[c].reshape(8 * 256, CW)
        hs[c] = mm(oga[Q : 2 * Q, :], wmat).astype(BF)
        cp = remote(hs.at[c], hr.at[c], h_send.at[c], h_recv.at[c], partner)
        cp.start()
        hsends.append(cp)
        hp[c] = mm(oga[0:Q, :], wmat)

    def head_grad(c):
        remote(hs.at[c], hr.at[c], h_send.at[c], h_recv.at[c], partner).wait_recv()
        g = (hp[c] + hr[c].astype(F32)).astype(BF)
        gg[:, cols(c)] = g
        wgc = (g.astype(F32) * ee[:, cols(c)]).astype(BF)
        wg[:, cols(c)] = wgc
        local = mm(cm, wgc, 0, 0)
        for k in range(2):
            al[c, k] = local[:, k * HW : (k + 1) * HW]
        al_copy(c).start()

    def within_grads(c):
        gc = gg[:, cols(c)]
        prod = mm(gc, xm[c], 1, 1)
        acc = skip_row[:, c * CW : (c + 1) * CW] * gc.astype(F32)
        tot = None
        for k in range(HC):
            h = c * HC + k
            paired = (wt[h] * prod[:, k * Q : (k + 1) * Q]).astype(BF).astype(F32)
            tot = paired if tot is None else tot + paired
            acc = acc + mm(mix[h], gc * masks[k], 0, 0)
        psum[...] = tot if c == 0 else psum[...] + tot
        gi[:, cols(c)] = acc

    def finish(c):
        ax_copy(c).wait_recv()
        gin_ref[:, cols(c)] = (gi[:, cols(c)] + te[:, cols(c)] * mm(bm, adt[c])).astype(BF)
        nb = mm(win[:, cols(c)], adt[c], 1, 1)
        nc = mm(wg[:, cols(c)], stt[c], 1, 1)
        gb_ref[...] = nb if c == 0 else gb_ref[...] + nb
        gc_ref[...] = nc if c == 0 else gc_ref[...] + nc

    dsends = []

    def dc_copy(c, r):
        return remote(ds.at[c, r], dr.at[c, r], dc_send.at[c, r], dc_recv.at[c, r], twin)

    def da_copy(c, k):
        return remote(
            da.at[c, pl.ds(k * HR, HR)], dar.at[c, k], da_send.at[c, k], da_recv.at[c, k], xdev(1 if k == 0 else 3)
        )

    def db_copy(c, k):
        return remote(db.at[c, k], dbr.at[c, k], db_send.at[c, k], db_recv.at[c, k], xdev(1 if k == 0 else 3))

    def begin(cp):
        cp.start()
        dsends.append(cp)

    def weight_partial(c):
        remote(outs.at[c, pl.ds(0, Q), :], outs.at[c, pl.ds(Q, Q), :], o_send.at[c], o_recv.at[c], partner).wait_recv()
        oc = outs[c]
        for r in (2, 1, 3, 0):
            ds[c, r] = mm(ogt[chip(r) * 2 + 1 - core], oc).astype(BF)
            begin(dc_copy(c, r))

    def weight_send(c):
        oc = outs[c]
        for r in (2, 1, 3, 0):
            own = mm(ogt[chip(r) * 2 + core], oc)
            dc_copy(c, r).wait_recv()
            both = own + dr[c, r].astype(F32)
            if r == 0:
                gw_ref[:, cols(c)] = both
            elif r == 2:
                da[c] = both.astype(BF)
                begin(da_copy(c, 0))
                begin(da_copy(c, 1))
            else:
                dk[c, r // 2] = both

    def weight_relay(c):
        for k in range(2):
            da_copy(c, k).wait_recv()
            both, part = dk[c, k], dar[c, k].astype(F32)
            rows = slice(k * HR, (k + 1) * HR)
            rest = slice((1 - k) * HR, (2 - k) * HR)
            db[c, k, rows, :] = (both[rows] + part).astype(BF)
            db[c, k, rest, :] = both[rest].astype(BF)
            begin(db_copy(c, k))

    def weight_sum(c):
        tot = gw_ref[:, cols(c)]
        for k in range(2):
            db_copy(c, k).wait_recv()
            tot = tot + dbr[c, k].astype(F32)
        gw_ref[:, cols(c)] = tot

    cx_copy.start()
    intra(0)
    states_send()
    send_w(2)
    send_w(3)
    relay_w(0)
    share_og(0)
    intra(1)
    relay_w(1)
    share_og(1)
    intra(2)
    states_done()
    relay_w(2)
    intra(3)
    sx_copy.wait_recv()
    output(0)
    output(1)
    output(2)
    output(3)
    relay_w(3)
    for cp in locs:
        cp.wait()
    share_w(0)
    share_w(1)
    for r in (1, 2, 3):
        frm = lax.rem(z + 4 - r, 4)
        for u in range(SUB):
            piece = oga.at[ogrows(frm, u), :]
            remote(piece, piece, oz_send.at[r - 1, u], oz_recv.at[r - 1, u], zdev(r)).wait_recv()
    head(0)
    for k in range(8):
        ogt[k] = jnp.transpose(oga[:, k * 256 : (k + 1) * 256])
    weight_partial(0)
    head(1)
    share_w(2)
    weight_partial(1)
    weight_send(0)
    head(2)
    share_w(3)
    weight_partial(2)
    weight_send(1)
    weight_relay(0)
    head(3)
    head_grad(0)
    weight_partial(3)
    weight_send(2)
    weight_relay(1)
    head_grad(1)
    adjoint_send(0)
    weight_send(3)
    weight_relay(2)
    head_grad(2)
    adjoint_send(1)
    adjoint_done(0)
    weight_relay(3)
    head_grad(3)
    adjoint_send(2)
    adjoint_done(1)
    within_grads(0)
    adjoint_send(3)
    adjoint_done(2)
    within_grads(1)
    finish(0)
    adjoint_done(3)
    within_grads(2)
    finish(1)
    within_grads(3)
    finish(2)
    finish(3)
    pb = psum[...].astype(BF)
    gb_ref[...] = gb_ref[...] + mm(pb, cm, 0, 0)
    gc_ref[...] = gc_ref[...] + mm(pb, bm)
    for c in range(CH):
        weight_sum(c)

    for cp in wsends + oysends + ozsends + fsends + osends + hsends + dsends:
        cp.wait_send()
    cx_copy.wait_send()
    sx_copy.wait_send()
    for c in range(CH):
        al_copy(c).wait_send()
        ax_copy(c).wait_send()
    for r in (1, 2, 3):

        @pl.when(x + r < 4)
        def _():
            f_copy(r).wait_send()

        @pl.when(x >= r)
        def _():
            for c in range(CH):
                a_copy(c, r).wait_send()


def hand_out(*refs):
    n = len(refs) // 2
    for k in range(n):
        refs[n + k][...] = refs[k][...]


def body(ssm_input, b_input, c_input, step_size, decay_rate, skip_gain, resets, out_grad, out_weight):
    vm, anym = pl.BlockSpec(memory_space=pltpu.VMEM), pl.BlockSpec(memory_space=pl.ANY)
    width = HEADS * PS
    dma = pltpu.SemaphoreType.DMA
    v = pltpu.VMEM
    HW = CW // 2
    scratch = [
        v((CH, 8, 256, CW), BF), v((2 * Q, 2048), BF), v((64, 2048), BF), v((8, 256, 2 * Q), BF),
        v((CH, HC * Q, CW), BF), v((HEADS, Q, Q), BF), v((HEADS, Q, Q), F32),
        v((Q, width), F32), v((Q, width), F32), v((Q, width), BF), v((Q, width), BF),
        v((CH, N, CW), BF), v((CH, N, CW), BF),
        v((Q, width), F32), v((CH, 2 * Q, CW), BF), v((CH, Q, CW), F32), v((CH, Q, CW), BF), v((CH, Q, CW), BF),
        v((Q, width), BF), v((Q, width), F32),
        v((2, CH, N + 8, HW), F32), v((CH, N + 8, HW), F32), v((CH, N + 16, HW), BF), v((3, CH, N + 16, HW), BF),
        v((CH, N, HW), F32), v((CH, N, HW), BF), v((CH, 2, N, HW), F32), v((CH, N, HW), F32),
        v((CH, N + 16, HW), BF), v((3, CH, N + 16, HW), BF), v((CH, N, HW), BF),
        v((CH, 4, 256, CW), BF), v((CH, 4, 256, CW), BF), v((CH, 256, CW), BF), v((CH, 2, 128, CW), BF),
        v((CH, 2, 256, CW), F32), v((CH, 2, 256, CW), BF), v((CH, 2, 256, CW), BF),
        v((128, Q), F32), v((Q, 128), F32), v((Q, Q), F32),
        dma((CH,)), dma((2, 8)), dma((CH, 2)), dma((CH, 2)), dma((CH, 2)), dma((CH, 2)), dma((CH, 4)), dma((CH, 4)),
        dma((SUB,)), dma((SUB,)), dma((3, SUB)), dma((3, SUB)),
        dma((1,)), dma((1,)), dma((3,)), dma((3,)), dma((1,)), dma((1,)),
        dma((CH,)), dma((CH,)), dma((CH, 3)), dma((CH, 3)), dma((CH,)), dma((CH,)),
        dma((CH,)), dma((CH,)), dma((CH,)), dma((CH,)), dma((CH, 4)), dma((CH, 4)),
        dma((CH, 2)), dma((CH, 2)), dma((CH, 2)), dma((CH, 2)),
    ]
    results = pl.pallas_call(
        kernel,
        out_shape=(
            jax.ShapeDtypeStruct((Q, width), BF),
            jax.ShapeDtypeStruct((Q, N), F32),
            jax.ShapeDtypeStruct((Q, N), F32),
            jax.ShapeDtypeStruct((256, width), F32),
        ),
        in_specs=[vm, vm, vm, vm, vm, vm, pl.BlockSpec(memory_space=pltpu.SMEM), anym, anym],
        out_specs=(vm, vm, vm, vm),
        scratch_shapes=scratch,
        compiler_params=pltpu.CompilerParams(
            collective_id=0, has_side_effects=True, vmem_limit_bytes=60 * 2**20
        ),
        name="block_backward",
    )(
        ssm_input[0], b_input[0], c_input[0], step_size[0], decay_rate.reshape(1, HEADS),
        skip_gain.reshape(1, HEADS), resets, out_grad[0], out_weight,
    )
    blocks = [pl.BlockSpec((64, a.shape[1]), lambda i: (i, 0)) for a in results]
    gin, gb, gc, gw = pl.pallas_call(
        hand_out,
        out_shape=[jax.ShapeDtypeStruct(a.shape, a.dtype) for a in results],
        grid=(4,),
        in_specs=blocks,
        out_specs=blocks,
        name="hand_out",
    )(*results)
    return gin[None], gb[None], gc[None], gw


def solution(mesh):
    in_specs = (
        P("dp", "seq", "tensor"),
        P("dp", "seq", "tensor"),
        P("dp", "seq", "tensor"),
        P("dp", "tensor", "seq"),
        P("tensor"),
        P("tensor"),
        P("dp", "seq"),
        P("dp", "seq", None),
        P(("seq", "dp"), "tensor"),
    )
    out_specs = (
        P("dp", "seq", "tensor"),
        P("dp", "seq", "tensor"),
        P("dp", "seq", "tensor"),
        P(("seq", "dp"), "tensor"),
    )
    return jax.shard_map(body, mesh=mesh, in_specs=in_specs, out_specs=out_specs, check_vma=False)
```

```python
import jax
import jax.numpy as jnp
from jax import lax
from jax.experimental import pallas as pl
from jax.experimental.pallas import tpu as pltpu
from jax.sharding import PartitionSpec as P

MESH = pl.DeviceIdType.MESH
BF = jnp.bfloat16
F32 = jnp.float32
Q, HEADS, PS, N = 256, 16, 64, 128
CH, HC, CW = 4, 4, 256
SUB = 4


def mm(a, b, ca=1, cb=0, precision=None):
    return lax.dot_general(
        a, b, (((ca,), (cb,)), ((), ())), preferred_element_type=F32, precision=precision
    )


def kernel(
    x_ref, b_ref, c_ref, step_ref, rate_ref, skip_ref, reset_ref, og_ref, w_ref,
    gin_ref, gb_ref, gc_ref, gw_ref,
    wb, oga, ogs, ogt, xm, mix, wt, ee, te, win, wg, stt, adt, yi, outs, hp, hs, hr, gg, gi,
    cx, cxr, fb, fbr, sacc, sx, al, alr, ab, abr, ax,
    ds, dr, da, dar, dk, db, dbr, rowbuf, colbuf, psum,
    loc_sem, ogl_sem, w_send, w_recv, wr_send, wr_recv, wc_send, wc_recv, oy_send, oy_recv, oz_send, oz_recv,
    cx_send, cx_recv, f_send, f_recv, sx_send, sx_recv, al_send, al_recv, a_send, a_recv, ax_send, ax_recv,
    o_send, o_recv, h_send, h_recv, dc_send, dc_recv, da_send, da_recv, db_send, db_recv,
):
    s, t, d = lax.axis_index("seq"), lax.axis_index("tensor"), lax.axis_index("dp")
    x, core = s // 2, lax.rem(s, 2)
    z, yl = t // 2, lax.rem(t, 2)

    def xdev(r):
        return (lax.rem(x + r, 4) * 2 + core, t, d)

    def zdev(r):
        return (s, lax.rem(z + r, 4) * 2 + yl, d)

    twin = (x * 2 + 1 - core, t, d)
    partner = (s, t, 1 - d)

    bar = pltpu.get_barrier_semaphore()
    peers = [xdev(1), xdev(2), xdev(3), zdev(1), zdev(2), zdev(3), twin, partner]
    for p in peers:
        pl.semaphore_signal(bar, inc=1, device_id=p, device_id_type=MESH)
    pl.semaphore_wait(bar, len(peers))

    def remote(src, dst, ssem, rsem, dev):
        return pltpu.make_async_remote_copy(
            src_ref=src, dst_ref=dst, send_sem=ssem, recv_sem=rsem, device_id=dev, device_id_type=MESH
        )

    def cols(c):
        return pl.ds(c * CW, CW)

    ogl = []
    for k in range(8):
        cp = pltpu.make_async_copy(
            og_ref.at[pl.ds(z * 64, 64), pl.ds((2 * k + 1 - d) * 256, 256)],
            ogs.at[:, pl.ds(k * 256, 256)], ogl_sem.at[0, k])
        cp.start()
        ogl.append(cp)
    wsends = []

    def w_copy(c, r):
        k = 0 if r == 1 else 1
        return remote(w_ref.at[:, cols(c)], wb.at[c, s], w_send.at[c, k], w_recv.at[c, k], xdev(r))

    def w_twin(c, j, frm):
        return remote(wb.at[c, frm], wb.at[c, frm], wc_send.at[c, j], wc_recv.at[c, j], twin)

    def send_w(c):
        own = remote(w_ref.at[:, cols(c)], wb.at[c, s], wc_send.at[c, 0], wc_recv.at[c, 0], twin)
        for cp in (w_copy(c, 1), w_copy(c, 3), own):
            cp.start()
            wsends.append(cp)

    for cp in ogl:
        cp.wait()
    RS = 64 // SUB

    def ogrows(zz, u):
        return pl.ds(Q + zz * 64 + u * RS, RS)

    oysends = []
    for u in range(SUB):
        cp = remote(ogs.at[pl.ds(u * RS, RS), :], oga.at[ogrows(z, u), :], oy_send.at[u], oy_recv.at[u], partner)
        cp.start()
        oysends.append(cp)
    send_w(0)
    locs = []
    for c in range(CH):
        cp = pltpu.make_async_copy(w_ref.at[:, cols(c)], wb.at[c, s], loc_sem.at[c])
        cp.start()
        locs.append(cp)
    for k in range(8):
        cp = pltpu.make_async_copy(
            og_ref.at[:, pl.ds((2 * k + d) * 256, 256)], oga.at[pl.ds(0, Q), pl.ds(k * 256, 256)], ogl_sem.at[1, k])
        cp.start()
        locs.append(cp)

    rate = rate_ref[...]
    eye = lax.broadcasted_iota(jnp.int32, (HEADS, HEADS), 0) == lax.broadcasted_iota(jnp.int32, (HEADS, HEADS), 1)
    rate_col = jnp.sum(jnp.where(eye, jnp.broadcast_to(rate, (HEADS, HEADS)), 0.0), axis=1, keepdims=True)
    run = -step_ref[...] * rate_col
    lane = lax.broadcasted_iota(jnp.int32, (HEADS, Q), 1)
    for k in range(8):
        run = run + jnp.where(lane >= (1 << k), pltpu.roll(run, 1 << k, 1), 0.0)
    rowbuf[...] = jnp.zeros_like(rowbuf)
    rowbuf[0:HEADS, :] = run
    lcol = jnp.transpose(rowbuf[...])
    colbuf[...] = lcol
    hrow = lax.broadcasted_iota(jnp.int32, (128, HEADS * PS), 0)
    hcol = lax.broadcasted_iota(jnp.int32, (128, HEADS * PS), 1) // PS
    spread = jnp.where(hrow == hcol, 1.0, 0.0).astype(F32)
    hi = lax.Precision.HIGHEST
    ee[...] = mm(jnp.exp(lcol), spread, precision=hi)
    te[...] = mm(jnp.exp(lcol[Q - 1 : Q, :] - lcol), spread, precision=hi)
    skip_row = mm(jnp.broadcast_to(skip_ref[...], (8, HEADS)), spread[0:HEADS, :], precision=hi)[0:1, :]
    keep = (1 - reset_ref[0, 0]).astype(F32)

    bm, cm = b_ref[...], c_ref[...]
    HW = CW // 2
    halves = [[slice(c * CW + k * HW, c * CW + (k + 1) * HW) for c in range(CH)] for k in range(2)]
    my_half = pl.ds(pl.multiple_of(core * HW, HW), HW)
    row8 = lax.broadcasted_iota(jnp.int32, (8, HW), 0)
    row16 = lax.broadcasted_iota(jnp.int32, (16, HW), 0)

    def cx_copy(c):
        return remote(cx.at[1 - core, c], cxr.at[c], cx_send.at[c], cx_recv.at[c], twin)

    def carry(c):
        win[:, cols(c)] = (x_ref[:, cols(c)].astype(F32) * te[:, cols(c)]).astype(BF)
        part = mm(bm, win[:, cols(c)], 0, 0)
        for k in range(2):
            cx[k, c, 0:N, :] = part[:, k * HW : (k + 1) * HW]
            gain = jnp.broadcast_to(ee[Q - 1 : Q, halves[k][c]], (8, HW))
            cx[k, c, N : N + 8, :] = jnp.where(row8 == 0, gain, keep)
        cx_copy(c).start()

    def first(a, b):
        return jnp.where(core == 0, a, b), jnp.where(core == 0, b, a)

    def gains(c):
        mine, its = cx[core, c, N : N + 8, :], cxr[c, N : N + 8, :]
        (d0, d1), (k0, k1) = first(mine[0:1], its[0:1]), first(mine[1:2], its[1:2])
        return d0, d1, k0, k1

    def message(ref, c, carry, gain):
        up = gain.astype(BF).astype(F32)
        ref[c, 0:N, :] = carry.astype(BF)
        ref[c, N : N + 16, :] = jnp.where(row16 == 0, up, jnp.where(row16 == 1, gain - up, 0.0)).astype(BF)

    def extend(ref, r, c, total):
        g = ref[r - 1, c, N : N + 16, :].astype(F32)
        return (g[0:1] + g[1:2]) * total + ref[r - 1, c, 0:N, :].astype(F32)

    def sx_copy(c):
        return remote(sx.at[c], stt.at[c, :, my_half], sx_send.at[c], sx_recv.at[c], twin)

    def f_copy(c, r):
        return remote(fb.at[c], fbr.at[r - 1, c], f_send.at[c, r - 1], f_recv.at[c, r - 1], xdev(r))

    def states_send(c):
        cx_copy(c).wait_recv()
        d0, d1, k0, k1 = gains(c)
        c0, c1 = first(cx[core, c, 0:N, :], cxr[c, 0:N, :])
        message(fb, c, d1 * k1 * c0 + c1, d1 * k1 * d0 * k0)
        for r in (1, 2, 3):

            @pl.when(x + r < 4)
            def _():
                f_copy(c, r).start()

    def states_done(c):
        sacc[c] = jnp.zeros((N, HW), F32)
        for r in (3, 2, 1):

            @pl.when(x >= r)
            def _():
                f_copy(c, r).wait_recv()
                sacc[c] = extend(fbr, r, c, sacc[c])

        d0, d1, k0, k1 = gains(c)
        c0, c1 = first(cx[core, c, 0:N, :], cxr[c, 0:N, :])
        st0 = k0 * sacc[c]
        st1 = k1 * (d0 * st0 + c0)
        mine, its = first(st0, st1)
        stt[c, :, my_half] = mine.astype(BF)
        sx[c] = its.astype(BF)
        sx_copy(c).start()

    def al_copy(c):
        return remote(al.at[c, 1 - core], alr.at[c], al_send.at[c], al_recv.at[c], twin)

    def a_copy(c, r):
        return remote(ab.at[c], abr.at[r - 1, c], a_send.at[c, r - 1], a_recv.at[c, r - 1], xdev(4 - r))

    def ax_copy(c):
        return remote(ax.at[c], adt.at[c, :, my_half], ax_send.at[c], ax_recv.at[c], twin)

    def adjoint_send(c):
        al_copy(c).wait_recv()
        d0, d1, k0, k1 = gains(c)
        a0, a1 = first(al[c, core], alr[c])
        message(ab, c, k0 * (d0 * k1 * a1 + a0), d1 * k1 * d0 * k0)
        for r in (1, 2, 3):

            @pl.when(x >= r)
            def _():
                a_copy(c, r).start()

    def adjoint_done(c):
        sacc[c] = jnp.zeros((N, HW), F32)
        for r in (3, 2, 1):

            @pl.when(x + r < 4)
            def _():
                a_copy(c, r).wait_recv()
                sacc[c] = extend(abr, r, c, sacc[c])

        d0, d1, k0, k1 = gains(c)
        a0, a1 = first(al[c, core], alr[c])
        ad1 = sacc[c]
        mine, its = first(k1 * (d1 * ad1 + a1), ad1)
        adt[c, :, my_half] = mine.astype(BF)
        ax[c] = its.astype(BF)
        ax_copy(c).start()

    scores = mm(cm, bm, 1, 1)
    ii = lax.broadcasted_iota(jnp.int32, (Q, Q), 0)
    jj = lax.broadcasted_iota(jnp.int32, (Q, Q), 1)
    causal = ii >= jj
    mlane = lax.broadcasted_iota(jnp.int32, (1, CW), 1) // PS
    masks = [jnp.where(mlane == k, 1.0, 0.0).astype(BF) for k in range(HC)]

    def intra(c):
        xc = x_ref[:, cols(c)]
        for k in range(HC):
            h = c * HC + k
            gap = colbuf[:, h : h + 1] - rowbuf[h : h + 1, :]
            w = jnp.where(causal, jnp.exp(jnp.minimum(gap, 0.0)), 0.0)
            wt[h] = w
            mix[h] = (w * scores).astype(BF)
            xm[c, k * Q : (k + 1) * Q, :] = xc * masks[k]
        acc = skip_row[:, c * CW : (c + 1) * CW] * xc.astype(F32)
        for k in range(HC):
            acc = acc + mm(mix[c * HC + k], xm[c, k * Q : (k + 1) * Q, :])
        yi[:, cols(c)] = acc

    ozsends = []

    def share_og(u):
        remote(ogs.at[pl.ds(u * RS, RS), :], oga.at[ogrows(z, u), :], oy_send.at[u], oy_recv.at[u], partner).wait_recv()
        for r in (1, 3, 2):
            piece = oga.at[ogrows(z, u), :]
            cp = remote(piece, piece, oz_send.at[r - 1, u], oz_recv.at[r - 1, u], zdev(r))
            cp.start()
            ozsends.append(cp)


    osends = []

    def output(c):
        sx_copy(c).wait_recv()
        o = yi[:, cols(c)] + ee[:, cols(c)] * mm(cm, stt[c])
        outs[c, 0:Q, :] = o.astype(BF)
        cp = remote(outs.at[c, pl.ds(0, Q), :], outs.at[c, pl.ds(Q, Q), :], o_send.at[c], o_recv.at[c], partner)
        cp.start()
        osends.append(cp)

    fsends = []
    HR = 128

    def chip(r):
        return lax.rem(x + r, 4)

    def wr_copy(c, k):
        rows = pl.ds(k * HR, HR)
        piece = wb.at[c, chip(3 if k == 0 else 1) * 2 + core, rows]
        return remote(piece, piece, wr_send.at[c, k], wr_recv.at[c, k], xdev(1 if k == 0 else 3))

    def relay_w(c):
        for k, r in ((0, 1), (1, 3)):
            w_copy(c, r).wait_recv()
            cp = wr_copy(c, k)
            cp.start()
            fsends.append(cp)
            cp = w_twin(c, 1 + k, chip(3 if k == 0 else 1) * 2 + core)
            cp.start()
            fsends.append(cp)

    def share_w(c):
        for k in range(2):
            wr_copy(c, k).wait_recv()
        cp = w_twin(c, 3, chip(2) * 2 + core)
        cp.start()
        fsends.append(cp)

    hsends = []

    def head(c):
        for j, r in enumerate((0, 3, 1, 2)):
            w_twin(c, j, chip(r) * 2 + 1 - core).wait_recv()
        wmat = wb[c].reshape(8 * 256, CW)
        hs[c] = mm(oga[Q : 2 * Q, :], wmat).astype(BF)
        cp = remote(hs.at[c], hr.at[c], h_send.at[c], h_recv.at[c], partner)
        cp.start()
        hsends.append(cp)
        hp[c] = mm(oga[0:Q, :], wmat)

    def head_grad(c):
        remote(hs.at[c], hr.at[c], h_send.at[c], h_recv.at[c], partner).wait_recv()
        g = (hp[c] + hr[c].astype(F32)).astype(BF)
        gg[:, cols(c)] = g
        wgc = (g.astype(F32) * ee[:, cols(c)]).astype(BF)
        wg[:, cols(c)] = wgc
        local = mm(cm, wgc, 0, 0)
        for k in range(2):
            al[c, k] = local[:, k * HW : (k + 1) * HW]
        al_copy(c).start()

    def within_grads(c):
        gc = gg[:, cols(c)]
        prod = mm(gc, xm[c], 1, 1)
        acc = skip_row[:, c * CW : (c + 1) * CW] * gc.astype(F32)
        tot = None
        for k in range(HC):
            h = c * HC + k
            paired = (wt[h] * prod[:, k * Q : (k + 1) * Q]).astype(BF).astype(F32)
            tot = paired if tot is None else tot + paired
            acc = acc + mm(mix[h], gc * masks[k], 0, 0)
        psum[...] = tot if c == 0 else psum[...] + tot
        gi[:, cols(c)] = acc

    def finish(c):
        ax_copy(c).wait_recv()
        gin_ref[:, cols(c)] = (gi[:, cols(c)] + te[:, cols(c)] * mm(bm, adt[c])).astype(BF)
        nb = mm(win[:, cols(c)], adt[c], 1, 1)
        nc = mm(wg[:, cols(c)], stt[c], 1, 1)
        gb_ref[...] = nb if c == 0 else gb_ref[...] + nb
        gc_ref[...] = nc if c == 0 else gc_ref[...] + nc

    dsends = []

    def dc_copy(c, r):
        return remote(ds.at[c, r], dr.at[c, r], dc_send.at[c, r], dc_recv.at[c, r], twin)

    def da_copy(c, k):
        return remote(
            da.at[c, pl.ds(k * HR, HR)], dar.at[c, k], da_send.at[c, k], da_recv.at[c, k], xdev(1 if k == 0 else 3)
        )

    def db_copy(c, k):
        return remote(db.at[c, k], dbr.at[c, k], db_send.at[c, k], db_recv.at[c, k], xdev(1 if k == 0 else 3))

    def begin(cp):
        cp.start()
        dsends.append(cp)

    def weight_partial(c):
        remote(outs.at[c, pl.ds(0, Q), :], outs.at[c, pl.ds(Q, Q), :], o_send.at[c], o_recv.at[c], partner).wait_recv()
        oc = outs[c]
        for r in (2, 1, 3, 0):
            ds[c, r] = mm(ogt[chip(r) * 2 + 1 - core], oc).astype(BF)
            begin(dc_copy(c, r))

    def weight_send(c):
        oc = outs[c]
        for r in (2, 1, 3, 0):
            own = mm(ogt[chip(r) * 2 + core], oc)
            dc_copy(c, r).wait_recv()
            both = own + dr[c, r].astype(F32)
            if r == 0:
                gw_ref[:, cols(c)] = both
            elif r == 2:
                da[c] = both.astype(BF)
                begin(da_copy(c, 0))
                begin(da_copy(c, 1))
            else:
                dk[c, r // 2] = both

    def weight_relay(c):
        for k in range(2):
            da_copy(c, k).wait_recv()
            both, part = dk[c, k], dar[c, k].astype(F32)
            rows = slice(k * HR, (k + 1) * HR)
            rest = slice((1 - k) * HR, (2 - k) * HR)
            db[c, k, rows, :] = (both[rows] + part).astype(BF)
            db[c, k, rest, :] = both[rest].astype(BF)
            begin(db_copy(c, k))

    def weight_sum(c):
        tot = gw_ref[:, cols(c)]
        for k in range(2):
            db_copy(c, k).wait_recv()
            tot = tot + dbr[c, k].astype(F32)
        gw_ref[:, cols(c)] = tot

    for c in range(CH):
        carry(c)
    states_send(0)
    states_send(1)
    states_send(2)
    states_send(3)
    intra(0)
    share_og(0)
    share_og(1)
    send_w(1)
    intra(1)
    states_done(0)
    relay_w(0)
    share_og(2)
    intra(2)
    states_done(1)
    send_w(2)
    output(0)
    share_og(3)
    intra(3)
    states_done(2)
    output(1)
    states_done(3)
    send_w(3)
    output(2)
    output(3)
    for cp in locs:
        cp.wait()
    share_w(0)
    relay_w(1)
    for r in (1, 2, 3):
        frm = lax.rem(z + 4 - r, 4)
        for u in range(SUB):
            piece = oga.at[ogrows(frm, u), :]
            remote(piece, piece, oz_send.at[r - 1, u], oz_recv.at[r - 1, u], zdev(r)).wait_recv()
    for k in range(8):
        ogt[k] = jnp.transpose(oga[:, k * 256 : (k + 1) * 256])
    weight_partial(0)
    relay_w(2)
    head(0)
    weight_send(0)
    relay_w(3)
    share_w(1)
    weight_partial(1)
    head(1)
    weight_send(1)
    weight_relay(0)
    share_w(2)
    weight_partial(2)
    head(2)
    weight_send(2)
    weight_relay(1)
    share_w(3)
    head(3)
    weight_partial(3)
    head_grad(0)
    adjoint_send(0)
    weight_send(3)
    weight_relay(2)
    head_grad(1)
    adjoint_send(1)
    head_grad(2)
    adjoint_done(0)
    adjoint_send(2)
    within_grads(0)
    head_grad(3)
    adjoint_send(3)
    weight_relay(3)
    adjoint_done(1)
    finish(0)
    within_grads(1)
    adjoint_done(2)
    finish(1)
    within_grads(2)
    finish(2)
    adjoint_done(3)
    within_grads(3)
    finish(3)
    weight_sum(0)
    weight_sum(1)
    pb = psum[...].astype(BF)
    gb_ref[...] = gb_ref[...] + mm(pb, cm, 0, 0)
    gc_ref[...] = gc_ref[...] + mm(pb, bm)
    weight_sum(2)
    weight_sum(3)

    for cp in wsends + oysends + ozsends + fsends + osends + hsends + dsends:
        cp.wait_send()
    for c in range(CH):
        cx_copy(c).wait_send()
        sx_copy(c).wait_send()
        al_copy(c).wait_send()
        ax_copy(c).wait_send()
    for r in (1, 2, 3):

        @pl.when(x + r < 4)
        def _():
            for c in range(CH):
                f_copy(c, r).wait_send()

        @pl.when(x >= r)
        def _():
            for c in range(CH):
                a_copy(c, r).wait_send()


def hand_out(*refs):
    n = len(refs) // 3
    src, dst, held, sem = refs[:n], refs[n : 2 * n], refs[2 * n : 3 * n], refs[3 * n]
    parts = [(k, pl.ds(i * 64, 64), sem.at[:, k, i]) for k in range(n) for i in range(4)]
    ins = [pltpu.make_async_copy(src[k].at[rows], held[k].at[rows], s.at[0]) for k, rows, s in parts]
    outs = [pltpu.make_async_copy(held[k].at[rows], dst[k].at[rows], s.at[1]) for k, rows, s in parts]
    for cp in ins:
        cp.start()
    for a, b in zip(ins, outs):
        a.wait()
        b.start()
    for cp in outs:
        cp.wait()


def body(ssm_input, b_input, c_input, step_size, decay_rate, skip_gain, resets, out_grad, out_weight):
    vm, anym = pl.BlockSpec(memory_space=pltpu.VMEM), pl.BlockSpec(memory_space=pl.ANY)
    width = HEADS * PS
    dma = pltpu.SemaphoreType.DMA
    v = pltpu.VMEM
    HW = CW // 2
    scratch = [
        v((CH, 8, 256, CW), BF), v((2 * Q, 2048), BF), v((64, 2048), BF), v((8, 256, 2 * Q), BF),
        v((CH, HC * Q, CW), BF), v((HEADS, Q, Q), BF), v((HEADS, Q, Q), F32),
        v((Q, width), F32), v((Q, width), F32), v((Q, width), BF), v((Q, width), BF),
        v((CH, N, CW), BF), v((CH, N, CW), BF),
        v((Q, width), F32), v((CH, 2 * Q, CW), BF), v((CH, Q, CW), F32), v((CH, Q, CW), BF), v((CH, Q, CW), BF),
        v((Q, width), BF), v((Q, width), F32),
        v((2, CH, N + 8, HW), F32), v((CH, N + 8, HW), F32), v((CH, N + 16, HW), BF), v((3, CH, N + 16, HW), BF),
        v((CH, N, HW), F32), v((CH, N, HW), BF), v((CH, 2, N, HW), F32), v((CH, N, HW), F32),
        v((CH, N + 16, HW), BF), v((3, CH, N + 16, HW), BF), v((CH, N, HW), BF),
        v((CH, 4, 256, CW), BF), v((CH, 4, 256, CW), BF), v((CH, 256, CW), BF), v((CH, 2, 128, CW), BF),
        v((CH, 2, 256, CW), F32), v((CH, 2, 256, CW), BF), v((CH, 2, 256, CW), BF),
        v((128, Q), F32), v((Q, 128), F32), v((Q, Q), F32),
        dma((CH,)), dma((2, 8)), dma((CH, 2)), dma((CH, 2)), dma((CH, 2)), dma((CH, 2)), dma((CH, 4)), dma((CH, 4)),
        dma((SUB,)), dma((SUB,)), dma((3, SUB)), dma((3, SUB)),
        dma((CH,)), dma((CH,)), dma((CH, 3)), dma((CH, 3)), dma((CH,)), dma((CH,)),
        dma((CH,)), dma((CH,)), dma((CH, 3)), dma((CH, 3)), dma((CH,)), dma((CH,)),
        dma((CH,)), dma((CH,)), dma((CH,)), dma((CH,)), dma((CH, 4)), dma((CH, 4)),
        dma((CH, 2)), dma((CH, 2)), dma((CH, 2)), dma((CH, 2)),
    ]
    results = pl.pallas_call(
        kernel,
        out_shape=(
            jax.ShapeDtypeStruct((Q, width), BF),
            jax.ShapeDtypeStruct((Q, N), F32),
            jax.ShapeDtypeStruct((Q, N), F32),
            jax.ShapeDtypeStruct((256, width), F32),
        ),
        in_specs=[vm, vm, vm, vm, vm, vm, pl.BlockSpec(memory_space=pltpu.SMEM), anym, anym],
        out_specs=(vm, vm, vm, vm),
        scratch_shapes=scratch,
        compiler_params=pltpu.CompilerParams(
            collective_id=0, has_side_effects=True, vmem_limit_bytes=60 * 2**20
        ),
        name="block_backward",
    )(
        ssm_input[0], b_input[0], c_input[0], step_size[0], decay_rate.reshape(1, HEADS),
        skip_gain.reshape(1, HEADS), resets, out_grad[0], out_weight,
    )
    gin, gb, gc, gw = pl.pallas_call(
        hand_out,
        out_shape=[jax.ShapeDtypeStruct(a.shape, a.dtype) for a in results],
        in_specs=[anym] * 4,
        out_specs=[anym] * 4,
        scratch_shapes=[v(a.shape, a.dtype) for a in results] + [dma((2, 4, 4))],
        name="hand_out",
    )(*results)
    return gin[None], gb[None], gc[None], gw


def solution(mesh):
    in_specs = (
        P("dp", "seq", "tensor"),
        P("dp", "seq", "tensor"),
        P("dp", "seq", "tensor"),
        P("dp", "tensor", "seq"),
        P("tensor"),
        P("tensor"),
        P("dp", "seq"),
        P("dp", "seq", None),
        P(("seq", "dp"), "tensor"),
    )
    out_specs = (
        P("dp", "seq", "tensor"),
        P("dp", "seq", "tensor"),
        P("dp", "seq", "tensor"),
        P(("seq", "dp"), "tensor"),
    )
    return jax.shard_map(body, mesh=mesh, in_specs=in_specs, out_specs=out_specs, check_vma=False)
```

```python
import jax
import jax.numpy as jnp
from jax import lax
from jax.experimental import pallas as pl
from jax.experimental.pallas import tpu as pltpu
from jax.sharding import PartitionSpec as P

MESH = pl.DeviceIdType.MESH
BF = jnp.bfloat16
F32 = jnp.float32
Q, HEADS, PS, N = 256, 16, 64, 128
CH, HC, CW = 4, 4, 256
SUB = 4


def mm(a, b, ca=1, cb=0, precision=None):
    return lax.dot_general(
        a, b, (((ca,), (cb,)), ((), ())), preferred_element_type=F32, precision=precision
    )


def kernel(
    x_ref, b_ref, c_ref, step_ref, rate_ref, skip_ref, reset_ref, og_ref, w_ref,
    gin_ref, gb_ref, gc_ref, gw_ref,
    wb, oga, ogs, ogt, xm, mix, wt, ee, te, win, wg, stt, adt, yi, outs, hp, hs, hr, gg, gi,
    cx, cxr, fb, fbr, sacc, sx, al, alr, ab, abr, ax,
    ds, dr, da, dar, dk, db, dbr, rowbuf, colbuf, psum,
    loc_sem, ogl_sem, w_send, w_recv, wr_send, wr_recv, wc_send, wc_recv, oy_send, oy_recv, oz_send, oz_recv,
    cx_send, cx_recv, f_send, f_recv, sx_send, sx_recv, al_send, al_recv, a_send, a_recv, ax_send, ax_recv,
    o_send, o_recv, h_send, h_recv, dc_send, dc_recv, da_send, da_recv, db_send, db_recv,
):
    s, t, d = lax.axis_index("seq"), lax.axis_index("tensor"), lax.axis_index("dp")
    x, core = s // 2, lax.rem(s, 2)
    z, yl = t // 2, lax.rem(t, 2)

    def xdev(r):
        return (lax.rem(x + r, 4) * 2 + core, t, d)

    def zdev(r):
        return (s, lax.rem(z + r, 4) * 2 + yl, d)

    twin = (x * 2 + 1 - core, t, d)
    partner = (s, t, 1 - d)

    bar = pltpu.get_barrier_semaphore()
    peers = [xdev(1), xdev(2), xdev(3), zdev(1), zdev(2), zdev(3), twin, partner]
    for p in peers:
        pl.semaphore_signal(bar, inc=1, device_id=p, device_id_type=MESH)

    def remote(src, dst, ssem, rsem, dev):
        return pltpu.make_async_remote_copy(
            src_ref=src, dst_ref=dst, send_sem=ssem, recv_sem=rsem, device_id=dev, device_id_type=MESH
        )

    def cols(c):
        return pl.ds(c * CW, CW)

    ogl = []
    for k in range(8):
        cp = pltpu.make_async_copy(
            og_ref.at[pl.ds(z * 64, 64), pl.ds((2 * k + 1 - d) * 256, 256)],
            ogs.at[:, pl.ds(k * 256, 256)], ogl_sem.at[0, k])
        cp.start()
        ogl.append(cp)
    wsends = []

    def w_copy(c, r):
        k = 0 if r == 1 else 1
        return remote(w_ref.at[:, cols(c)], wb.at[c, s], w_send.at[c, k], w_recv.at[c, k], xdev(r))

    def w_twin(c, j, frm):
        return remote(wb.at[c, frm], wb.at[c, frm], wc_send.at[c, j], wc_recv.at[c, j], twin)

    def send_w(c):
        own = remote(w_ref.at[:, cols(c)], wb.at[c, s], wc_send.at[c, 0], wc_recv.at[c, 0], twin)
        for cp in (w_copy(c, 1), w_copy(c, 3), own):
            cp.start()
            wsends.append(cp)

    RS = 64 // SUB

    def ogrows(zz, u):
        return pl.ds(Q + zz * 64 + u * RS, RS)

    locs = []
    for c in range(CH):
        cp = pltpu.make_async_copy(w_ref.at[:, cols(c)], wb.at[c, s], loc_sem.at[c])
        cp.start()
        locs.append(cp)
    for k in range(8):
        cp = pltpu.make_async_copy(
            og_ref.at[:, pl.ds((2 * k + d) * 256, 256)], oga.at[pl.ds(0, Q), pl.ds(k * 256, 256)], ogl_sem.at[1, k])
        cp.start()
        locs.append(cp)

    rate = rate_ref[...]
    eye = lax.broadcasted_iota(jnp.int32, (HEADS, HEADS), 0) == lax.broadcasted_iota(jnp.int32, (HEADS, HEADS), 1)
    rate_col = jnp.sum(jnp.where(eye, jnp.broadcast_to(rate, (HEADS, HEADS)), 0.0), axis=1, keepdims=True)
    run = -step_ref[...] * rate_col
    lane = lax.broadcasted_iota(jnp.int32, (HEADS, Q), 1)
    for k in range(8):
        run = run + jnp.where(lane >= (1 << k), pltpu.roll(run, 1 << k, 1), 0.0)
    rowbuf[...] = jnp.zeros_like(rowbuf)
    rowbuf[0:HEADS, :] = run
    lcol = jnp.transpose(rowbuf[...])
    colbuf[...] = lcol
    hrow = lax.broadcasted_iota(jnp.int32, (128, HEADS * PS), 0)
    hcol = lax.broadcasted_iota(jnp.int32, (128, HEADS * PS), 1) // PS
    spread = jnp.where(hrow == hcol, 1.0, 0.0).astype(F32)
    hi = lax.Precision.HIGHEST
    ee[...] = mm(jnp.exp(lcol), spread, precision=hi)
    te[...] = mm(jnp.exp(lcol[Q - 1 : Q, :] - lcol), spread, precision=hi)
    skip_row = mm(jnp.broadcast_to(skip_ref[...], (8, HEADS)), spread[0:HEADS, :], precision=hi)[0:1, :]
    keep = (1 - reset_ref[0, 0]).astype(F32)

    bm, cm = b_ref[...], c_ref[...]
    HW = CW // 2
    halves = [[slice(c * CW + k * HW, c * CW + (k + 1) * HW) for c in range(CH)] for k in range(2)]
    my_half = pl.ds(pl.multiple_of(core * HW, HW), HW)
    row8 = lax.broadcasted_iota(jnp.int32, (8, HW), 0)
    row16 = lax.broadcasted_iota(jnp.int32, (16, HW), 0)

    def cx_copy(c):
        return remote(cx.at[1 - core, c], cxr.at[c], cx_send.at[c], cx_recv.at[c], twin)

    def carry(c):
        win[:, cols(c)] = (x_ref[:, cols(c)].astype(F32) * te[:, cols(c)]).astype(BF)
        part = mm(bm, win[:, cols(c)], 0, 0)
        for k in range(2):
            cx[k, c, 0:N, :] = part[:, k * HW : (k + 1) * HW]
            gain = jnp.broadcast_to(ee[Q - 1 : Q, halves[k][c]], (8, HW))
            cx[k, c, N : N + 8, :] = jnp.where(row8 == 0, gain, keep)

    def first(a, b):
        return jnp.where(core == 0, a, b), jnp.where(core == 0, b, a)

    def gains(c):
        mine, its = cx[core, c, N : N + 8, :], cxr[c, N : N + 8, :]
        (d0, d1), (k0, k1) = first(mine[0:1], its[0:1]), first(mine[1:2], its[1:2])
        return d0, d1, k0, k1

    def message(ref, c, carry, gain):
        up = gain.astype(BF).astype(F32)
        ref[c, 0:N, :] = carry.astype(BF)
        ref[c, N : N + 16, :] = jnp.where(row16 == 0, up, jnp.where(row16 == 1, gain - up, 0.0)).astype(BF)

    def extend(ref, r, c, total):
        g = ref[r - 1, c, N : N + 16, :].astype(F32)
        return (g[0:1] + g[1:2]) * total + ref[r - 1, c, 0:N, :].astype(F32)

    def sx_copy(c):
        return remote(sx.at[c], stt.at[c, :, my_half], sx_send.at[c], sx_recv.at[c], twin)

    def f_copy(c, r):
        return remote(fb.at[c], fbr.at[r - 1, c], f_send.at[c, r - 1], f_recv.at[c, r - 1], xdev(r))

    def states_send(c):
        cx_copy(c).wait_recv()
        d0, d1, k0, k1 = gains(c)
        c0, c1 = first(cx[core, c, 0:N, :], cxr[c, 0:N, :])
        message(fb, c, d1 * k1 * c0 + c1, d1 * k1 * d0 * k0)
        for r in (1, 2, 3):

            @pl.when(x + r < 4)
            def _():
                f_copy(c, r).start()

    def states_done(c):
        sacc[c] = jnp.zeros((N, HW), F32)
        for r in (3, 2, 1):

            @pl.when(x >= r)
            def _():
                f_copy(c, r).wait_recv()
                sacc[c] = extend(fbr, r, c, sacc[c])

        d0, d1, k0, k1 = gains(c)
        c0, c1 = first(cx[core, c, 0:N, :], cxr[c, 0:N, :])
        st0 = k0 * sacc[c]
        st1 = k1 * (d0 * st0 + c0)
        mine, its = first(st0, st1)
        stt[c, :, my_half] = mine.astype(BF)
        sx[c] = its.astype(BF)
        sx_copy(c).start()

    def al_copy(c):
        return remote(al.at[c, 1 - core], alr.at[c], al_send.at[c], al_recv.at[c], twin)

    def a_copy(c, r):
        return remote(ab.at[c], abr.at[r - 1, c], a_send.at[c, r - 1], a_recv.at[c, r - 1], xdev(4 - r))

    def ax_copy(c):
        return remote(ax.at[c], adt.at[c, :, my_half], ax_send.at[c], ax_recv.at[c], twin)

    def adjoint_send(c):
        al_copy(c).wait_recv()
        d0, d1, k0, k1 = gains(c)
        a0, a1 = first(al[c, core], alr[c])
        message(ab, c, k0 * (d0 * k1 * a1 + a0), d1 * k1 * d0 * k0)
        for r in (1, 2, 3):

            @pl.when(x >= r)
            def _():
                a_copy(c, r).start()

    def adjoint_done(c):
        sacc[c] = jnp.zeros((N, HW), F32)
        for r in (3, 2, 1):

            @pl.when(x + r < 4)
            def _():
                a_copy(c, r).wait_recv()
                sacc[c] = extend(abr, r, c, sacc[c])

        d0, d1, k0, k1 = gains(c)
        a0, a1 = first(al[c, core], alr[c])
        ad1 = sacc[c]
        mine, its = first(k1 * (d1 * ad1 + a1), ad1)
        adt[c, :, my_half] = mine.astype(BF)
        ax[c] = its.astype(BF)
        ax_copy(c).start()

    scores = mm(cm, bm, 1, 1)
    ii = lax.broadcasted_iota(jnp.int32, (Q, Q), 0)
    jj = lax.broadcasted_iota(jnp.int32, (Q, Q), 1)
    causal = ii >= jj
    mlane = lax.broadcasted_iota(jnp.int32, (1, CW), 1) // PS
    masks = [jnp.where(mlane == k, 1.0, 0.0).astype(BF) for k in range(HC)]

    def intra(c):
        xc = x_ref[:, cols(c)]
        for k in range(HC):
            h = c * HC + k
            gap = colbuf[:, h : h + 1] - rowbuf[h : h + 1, :]
            w = jnp.where(causal, jnp.exp(jnp.minimum(gap, 0.0)), 0.0)
            wt[h] = w
            mix[h] = (w * scores).astype(BF)
            xm[c, k * Q : (k + 1) * Q, :] = xc * masks[k]
        acc = skip_row[:, c * CW : (c + 1) * CW] * xc.astype(F32)
        for k in range(HC):
            acc = acc + mm(mix[c * HC + k], xm[c, k * Q : (k + 1) * Q, :])
        yi[:, cols(c)] = acc

    ozsends = []

    def share_og(u):
        remote(ogs.at[pl.ds(u * RS, RS), :], oga.at[ogrows(z, u), :], oy_send.at[u], oy_recv.at[u], partner).wait_recv()
        for r in (1, 3, 2):
            piece = oga.at[ogrows(z, u), :]
            cp = remote(piece, piece, oz_send.at[r - 1, u], oz_recv.at[r - 1, u], zdev(r))
            cp.start()
            ozsends.append(cp)


    osends = []

    def output(c):
        sx_copy(c).wait_recv()
        o = yi[:, cols(c)] + ee[:, cols(c)] * mm(cm, stt[c])
        outs[c, 0:Q, :] = o.astype(BF)
        cp = remote(outs.at[c, pl.ds(0, Q), :], outs.at[c, pl.ds(Q, Q), :], o_send.at[c], o_recv.at[c], partner)
        cp.start()
        osends.append(cp)

    fsends = []
    HR = 128

    def chip(r):
        return lax.rem(x + r, 4)

    def wr_copy(c, k):
        rows = pl.ds(k * HR, HR)
        piece = wb.at[c, chip(3 if k == 0 else 1) * 2 + core, rows]
        return remote(piece, piece, wr_send.at[c, k], wr_recv.at[c, k], xdev(1 if k == 0 else 3))

    def relay_w(c):
        for k, r in ((0, 1), (1, 3)):
            w_copy(c, r).wait_recv()
            cp = wr_copy(c, k)
            cp.start()
            fsends.append(cp)
            cp = w_twin(c, 1 + k, chip(3 if k == 0 else 1) * 2 + core)
            cp.start()
            fsends.append(cp)

    def share_w(c):
        for k in range(2):
            wr_copy(c, k).wait_recv()
        cp = w_twin(c, 3, chip(2) * 2 + core)
        cp.start()
        fsends.append(cp)

    hsends = []

    def head(c):
        for j, r in enumerate((0, 3, 1, 2)):
            w_twin(c, j, chip(r) * 2 + 1 - core).wait_recv()
        wmat = wb[c].reshape(8 * 256, CW)
        hs[c] = mm(oga[Q : 2 * Q, :], wmat).astype(BF)
        cp = remote(hs.at[c], hr.at[c], h_send.at[c], h_recv.at[c], partner)
        cp.start()
        hsends.append(cp)
        hp[c] = mm(oga[0:Q, :], wmat)

    def head_grad(c):
        remote(hs.at[c], hr.at[c], h_send.at[c], h_recv.at[c], partner).wait_recv()
        g = (hp[c] + hr[c].astype(F32)).astype(BF)
        gg[:, cols(c)] = g
        wgc = (g.astype(F32) * ee[:, cols(c)]).astype(BF)
        wg[:, cols(c)] = wgc
        local = mm(cm, wgc, 0, 0)
        for k in range(2):
            al[c, k] = local[:, k * HW : (k + 1) * HW]
        al_copy(c).start()

    def within_grads(c):
        gc = gg[:, cols(c)]
        prod = mm(gc, xm[c], 1, 1)
        acc = skip_row[:, c * CW : (c + 1) * CW] * gc.astype(F32)
        tot = None
        for k in range(HC):
            h = c * HC + k
            paired = (wt[h] * prod[:, k * Q : (k + 1) * Q]).astype(BF).astype(F32)
            tot = paired if tot is None else tot + paired
            acc = acc + mm(mix[h], gc * masks[k], 0, 0)
        psum[...] = tot if c == 0 else psum[...] + tot
        gi[:, cols(c)] = acc

    def finish(c):
        ax_copy(c).wait_recv()
        gin_ref[:, cols(c)] = (gi[:, cols(c)] + te[:, cols(c)] * mm(bm, adt[c])).astype(BF)
        nb = mm(win[:, cols(c)], adt[c], 1, 1)
        nc = mm(wg[:, cols(c)], stt[c], 1, 1)
        gb_ref[...] = nb if c == 0 else gb_ref[...] + nb
        gc_ref[...] = nc if c == 0 else gc_ref[...] + nc

    dsends = []

    def dc_copy(c, r):
        return remote(ds.at[c, r], dr.at[c, r], dc_send.at[c, r], dc_recv.at[c, r], twin)

    def da_copy(c, k):
        return remote(
            da.at[c, pl.ds(k * HR, HR)], dar.at[c, k], da_send.at[c, k], da_recv.at[c, k], xdev(1 if k == 0 else 3)
        )

    def db_copy(c, k):
        return remote(db.at[c, k], dbr.at[c, k], db_send.at[c, k], db_recv.at[c, k], xdev(1 if k == 0 else 3))

    def begin(cp):
        cp.start()
        dsends.append(cp)

    def turn(k):
        ogt[k, :, Q : 2 * Q] = jnp.transpose(oga[Q : 2 * Q, pl.ds(pl.multiple_of(k * 256, 256), 256)])

    def weight_partial(c):
        remote(outs.at[c, pl.ds(0, Q), :], outs.at[c, pl.ds(Q, Q), :], o_send.at[c], o_recv.at[c], partner).wait_recv()
        oc = outs[c]
        for r in (2, 1, 3, 0):
            block = chip(r) * 2 + 1 - core
            if c == 0:
                turn(block)
            ds[c, r] = mm(ogt[block], oc).astype(BF)
            begin(dc_copy(c, r))

    def weight_send(c):
        oc = outs[c]
        for r in (2, 1, 3, 0):
            block = chip(r) * 2 + core
            if c == 0:
                turn(block)
            own = mm(ogt[block], oc)
            dc_copy(c, r).wait_recv()
            both = own + dr[c, r].astype(F32)
            if r == 0:
                gw_ref[:, cols(c)] = both
            elif r == 2:
                da[c] = both.astype(BF)
                begin(da_copy(c, 0))
                begin(da_copy(c, 1))
            else:
                dk[c, r // 2] = both

    def weight_relay(c):
        for k in range(2):
            da_copy(c, k).wait_recv()
            both, part = dk[c, k], dar[c, k].astype(F32)
            rows = slice(k * HR, (k + 1) * HR)
            rest = slice((1 - k) * HR, (2 - k) * HR)
            db[c, k, rows, :] = (both[rows] + part).astype(BF)
            db[c, k, rest, :] = both[rest].astype(BF)
            begin(db_copy(c, k))

    def weight_sum(c):
        tot = gw_ref[:, cols(c)]
        for k in range(2):
            db_copy(c, k).wait_recv()
            tot = tot + dbr[c, k].astype(F32)
        gw_ref[:, cols(c)] = tot

    for c in range(CH):
        carry(c)
    pl.semaphore_wait(bar, len(peers))
    for c in range(CH):
        cx_copy(c).start()
    for cp in ogl:
        cp.wait()
    oysends = []
    for u in range(SUB):
        cp = remote(ogs.at[pl.ds(u * RS, RS), :], oga.at[ogrows(z, u), :], oy_send.at[u], oy_recv.at[u], partner)
        cp.start()
        oysends.append(cp)
    send_w(0)
    states_send(0)
    states_send(1)
    states_send(2)
    states_send(3)
    intra(0)
    share_og(0)
    share_og(1)
    send_w(1)
    intra(1)
    states_done(0)
    relay_w(0)
    share_og(2)
    intra(2)
    states_done(1)
    send_w(2)
    output(0)
    share_og(3)
    intra(3)
    states_done(2)
    output(1)
    states_done(3)
    send_w(3)
    output(2)
    output(3)
    for cp in locs:
        cp.wait()
    for k in range(8):
        ogt[k, :, 0:Q] = jnp.transpose(oga[0:Q, k * 256 : (k + 1) * 256])
    share_w(0)
    relay_w(1)
    for r in (1, 2, 3):
        frm = lax.rem(z + 4 - r, 4)
        for u in range(SUB):
            piece = oga.at[ogrows(frm, u), :]
            remote(piece, piece, oz_send.at[r - 1, u], oz_recv.at[r - 1, u], zdev(r)).wait_recv()
    weight_partial(0)
    relay_w(2)
    head(0)
    weight_send(0)
    relay_w(3)
    share_w(1)
    weight_partial(1)
    head(1)
    weight_send(1)
    weight_relay(0)
    share_w(2)
    weight_partial(2)
    head(2)
    weight_send(2)
    weight_relay(1)
    share_w(3)
    head(3)
    weight_partial(3)
    head_grad(0)
    adjoint_send(0)
    weight_send(3)
    weight_relay(2)
    head_grad(1)
    adjoint_send(1)
    head_grad(2)
    adjoint_done(0)
    adjoint_send(2)
    within_grads(0)
    head_grad(3)
    adjoint_send(3)
    weight_relay(3)
    adjoint_done(1)
    finish(0)
    within_grads(1)
    adjoint_done(2)
    finish(1)
    within_grads(2)
    finish(2)
    adjoint_done(3)
    within_grads(3)
    finish(3)
    weight_sum(0)
    weight_sum(1)
    pb = psum[...].astype(BF)
    gb_ref[...] = gb_ref[...] + mm(pb, cm, 0, 0)
    gc_ref[...] = gc_ref[...] + mm(pb, bm)
    weight_sum(2)
    weight_sum(3)

    for cp in wsends + oysends + ozsends + fsends + osends + hsends + dsends:
        cp.wait_send()
    for c in range(CH):
        cx_copy(c).wait_send()
        sx_copy(c).wait_send()
        al_copy(c).wait_send()
        ax_copy(c).wait_send()
    for r in (1, 2, 3):

        @pl.when(x + r < 4)
        def _():
            for c in range(CH):
                f_copy(c, r).wait_send()

        @pl.when(x >= r)
        def _():
            for c in range(CH):
                a_copy(c, r).wait_send()


def hand_out(*refs):
    n = len(refs) // 3
    src, dst, held, sem = refs[:n], refs[n : 2 * n], refs[2 * n : 3 * n], refs[3 * n]
    parts = [(k, pl.ds(i * 64, 64), sem.at[:, k, i]) for k in range(n) for i in range(4)]
    ins = [pltpu.make_async_copy(src[k].at[rows], held[k].at[rows], s.at[0]) for k, rows, s in parts]
    outs = [pltpu.make_async_copy(held[k].at[rows], dst[k].at[rows], s.at[1]) for k, rows, s in parts]
    for cp in ins:
        cp.start()
    for a, b in zip(ins, outs):
        a.wait()
        b.start()
    for cp in outs:
        cp.wait()


def body(ssm_input, b_input, c_input, step_size, decay_rate, skip_gain, resets, out_grad, out_weight):
    vm, anym = pl.BlockSpec(memory_space=pltpu.VMEM), pl.BlockSpec(memory_space=pl.ANY)
    width = HEADS * PS
    dma = pltpu.SemaphoreType.DMA
    v = pltpu.VMEM
    HW = CW // 2
    scratch = [
        v((CH, 8, 256, CW), BF), v((2 * Q, 2048), BF), v((64, 2048), BF), v((8, 256, 2 * Q), BF),
        v((CH, HC * Q, CW), BF), v((HEADS, Q, Q), BF), v((HEADS, Q, Q), F32),
        v((Q, width), F32), v((Q, width), F32), v((Q, width), BF), v((Q, width), BF),
        v((CH, N, CW), BF), v((CH, N, CW), BF),
        v((Q, width), F32), v((CH, 2 * Q, CW), BF), v((CH, Q, CW), F32), v((CH, Q, CW), BF), v((CH, Q, CW), BF),
        v((Q, width), BF), v((Q, width), F32),
        v((2, CH, N + 8, HW), F32), v((CH, N + 8, HW), F32), v((CH, N + 16, HW), BF), v((3, CH, N + 16, HW), BF),
        v((CH, N, HW), F32), v((CH, N, HW), BF), v((CH, 2, N, HW), F32), v((CH, N, HW), F32),
        v((CH, N + 16, HW), BF), v((3, CH, N + 16, HW), BF), v((CH, N, HW), BF),
        v((CH, 4, 256, CW), BF), v((CH, 4, 256, CW), BF), v((CH, 256, CW), BF), v((CH, 2, 128, CW), BF),
        v((CH, 2, 256, CW), F32), v((CH, 2, 256, CW), BF), v((CH, 2, 256, CW), BF),
        v((128, Q), F32), v((Q, 128), F32), v((Q, Q), F32),
        dma((CH,)), dma((2, 8)), dma((CH, 2)), dma((CH, 2)), dma((CH, 2)), dma((CH, 2)), dma((CH, 4)), dma((CH, 4)),
        dma((SUB,)), dma((SUB,)), dma((3, SUB)), dma((3, SUB)),
        dma((CH,)), dma((CH,)), dma((CH, 3)), dma((CH, 3)), dma((CH,)), dma((CH,)),
        dma((CH,)), dma((CH,)), dma((CH, 3)), dma((CH, 3)), dma((CH,)), dma((CH,)),
        dma((CH,)), dma((CH,)), dma((CH,)), dma((CH,)), dma((CH, 4)), dma((CH, 4)),
        dma((CH, 2)), dma((CH, 2)), dma((CH, 2)), dma((CH, 2)),
    ]
    results = pl.pallas_call(
        kernel,
        out_shape=(
            jax.ShapeDtypeStruct((Q, width), BF),
            jax.ShapeDtypeStruct((Q, N), F32),
            jax.ShapeDtypeStruct((Q, N), F32),
            jax.ShapeDtypeStruct((256, width), F32),
        ),
        in_specs=[vm, vm, vm, vm, vm, vm, pl.BlockSpec(memory_space=pltpu.SMEM), anym, anym],
        out_specs=(vm, vm, vm, vm),
        scratch_shapes=scratch,
        compiler_params=pltpu.CompilerParams(
            collective_id=0, has_side_effects=True, vmem_limit_bytes=60 * 2**20
        ),
        name="block_backward",
    )(
        ssm_input[0], b_input[0], c_input[0], step_size[0], decay_rate.reshape(1, HEADS),
        skip_gain.reshape(1, HEADS), resets, out_grad[0], out_weight,
    )
    gin, gb, gc, gw = pl.pallas_call(
        hand_out,
        out_shape=[jax.ShapeDtypeStruct(a.shape, a.dtype) for a in results],
        in_specs=[anym] * 4,
        out_specs=[anym] * 4,
        scratch_shapes=[v(a.shape, a.dtype) for a in results] + [dma((2, 4, 4))],
        name="hand_out",
    )(*results)
    return gin[None], gb[None], gc[None], gw


def solution(mesh):
    in_specs = (
        P("dp", "seq", "tensor"),
        P("dp", "seq", "tensor"),
        P("dp", "seq", "tensor"),
        P("dp", "tensor", "seq"),
        P("tensor"),
        P("tensor"),
        P("dp", "seq"),
        P("dp", "seq", None),
        P(("seq", "dp"), "tensor"),
    )
    out_specs = (
        P("dp", "seq", "tensor"),
        P("dp", "seq", "tensor"),
        P("dp", "seq", "tensor"),
        P(("seq", "dp"), "tensor"),
    )
    return jax.shard_map(body, mesh=mesh, in_specs=in_specs, out_specs=out_specs, check_vma=False)
```

```python
import jax
import jax.numpy as jnp
from jax import lax
from jax.experimental import pallas as pl
from jax.experimental.pallas import tpu as pltpu
from jax.sharding import PartitionSpec as P

MESH = pl.DeviceIdType.MESH
BF = jnp.bfloat16
F32 = jnp.float32
Q, HEADS, PS, N = 256, 16, 64, 128
CH, HC, CW = 4, 4, 256
SUB = 4


def mm(a, b, ca=1, cb=0, precision=None):
    return lax.dot_general(
        a, b, (((ca,), (cb,)), ((), ())), preferred_element_type=F32, precision=precision
    )


def kernel(
    x_ref, b_ref, c_ref, step_ref, rate_ref, skip_ref, reset_ref, og_ref, w_ref,
    gin_ref, gb_ref, gc_ref, gw_ref,
    wb, oga, ogs, ogt, xm, mix, wt, ee, te, win, wg, stt, adt, yi, outs, hp, hs, hr, gg, gi,
    cx, cxr, fb, fbr, sacc, sx, al, alr, ab, abr, ax,
    ds, dr, da, dar, dk, db, dbr, rowbuf, colbuf, psum,
    loc_sem, ogl_sem, w_send, w_recv, wr_send, wr_recv, wc_send, wc_recv, oy_send, oy_recv, oz_send, oz_recv,
    cx_send, cx_recv, f_send, f_recv, sx_send, sx_recv, al_send, al_recv, a_send, a_recv, ax_send, ax_recv,
    o_send, o_recv, h_send, h_recv, dc_send, dc_recv, da_send, da_recv, db_send, db_recv,
):
    s, t, d = lax.axis_index("seq"), lax.axis_index("tensor"), lax.axis_index("dp")
    x, core = s // 2, lax.rem(s, 2)
    z, yl = t // 2, lax.rem(t, 2)

    def xdev(r):
        return (lax.rem(x + r, 4) * 2 + core, t, d)

    def zdev(r):
        return (s, lax.rem(z + r, 4) * 2 + yl, d)

    twin = (x * 2 + 1 - core, t, d)
    partner = (s, t, 1 - d)

    bar = pltpu.get_barrier_semaphore()
    peers = [xdev(1), xdev(2), xdev(3), zdev(1), zdev(2), zdev(3), twin, partner]
    for p in peers:
        pl.semaphore_signal(bar, inc=1, device_id=p, device_id_type=MESH)

    def remote(src, dst, ssem, rsem, dev):
        return pltpu.make_async_remote_copy(
            src_ref=src, dst_ref=dst, send_sem=ssem, recv_sem=rsem, device_id=dev, device_id_type=MESH
        )

    def cols(c):
        return pl.ds(c * CW, CW)

    ogl = []
    for k in range(8):
        cp = pltpu.make_async_copy(
            og_ref.at[pl.ds(z * 64, 64), pl.ds((2 * k + 1 - d) * 256, 256)],
            ogs.at[:, pl.ds(k * 256, 256)], ogl_sem.at[0, k])
        cp.start()
        ogl.append(cp)
    wsends = []

    def w_copy(c, r):
        k = 0 if r == 1 else 1
        return remote(w_ref.at[:, cols(c)], wb.at[c, s], w_send.at[c, k], w_recv.at[c, k], xdev(r))

    def w_twin(c, j, frm):
        return remote(wb.at[c, frm], wb.at[c, frm], wc_send.at[c, j], wc_recv.at[c, j], twin)

    def send_w(c):
        own = remote(w_ref.at[:, cols(c)], wb.at[c, s], wc_send.at[c, 0], wc_recv.at[c, 0], twin)
        for cp in (w_copy(c, 1), w_copy(c, 3), own):
            cp.start()
            wsends.append(cp)

    RS = 64 // SUB

    def ogrows(zz, u):
        return pl.ds(Q + zz * 64 + u * RS, RS)

    locs = []
    for c in range(CH):
        cp = pltpu.make_async_copy(w_ref.at[:, cols(c)], wb.at[c, s], loc_sem.at[c])
        cp.start()
        locs.append(cp)
    for k in range(8):
        cp = pltpu.make_async_copy(
            og_ref.at[:, pl.ds((2 * k + d) * 256, 256)], oga.at[pl.ds(0, Q), pl.ds(k * 256, 256)], ogl_sem.at[1, k])
        cp.start()
        locs.append(cp)

    rate = rate_ref[...]
    eye = lax.broadcasted_iota(jnp.int32, (HEADS, HEADS), 0) == lax.broadcasted_iota(jnp.int32, (HEADS, HEADS), 1)
    rate_col = jnp.sum(jnp.where(eye, jnp.broadcast_to(rate, (HEADS, HEADS)), 0.0), axis=1, keepdims=True)
    run = -step_ref[...] * rate_col
    lane = lax.broadcasted_iota(jnp.int32, (HEADS, Q), 1)
    for k in range(8):
        run = run + jnp.where(lane >= (1 << k), pltpu.roll(run, 1 << k, 1), 0.0)
    rowbuf[...] = jnp.zeros_like(rowbuf)
    rowbuf[0:HEADS, :] = run
    lcol = jnp.transpose(rowbuf[...])
    colbuf[...] = lcol
    hrow = lax.broadcasted_iota(jnp.int32, (128, HEADS * PS), 0)
    hcol = lax.broadcasted_iota(jnp.int32, (128, HEADS * PS), 1) // PS
    spread = jnp.where(hrow == hcol, 1.0, 0.0).astype(F32)
    hi = lax.Precision.HIGHEST
    ee[...] = mm(jnp.exp(lcol), spread, precision=hi)
    te[...] = mm(jnp.exp(lcol[Q - 1 : Q, :] - lcol), spread, precision=hi)
    skip_row = mm(jnp.broadcast_to(skip_ref[...], (8, HEADS)), spread[0:HEADS, :], precision=hi)[0:1, :]
    keep = (1 - reset_ref[0, 0]).astype(F32)

    bm, cm = b_ref[...], c_ref[...]
    HW = CW // 2
    halves = [[slice(c * CW + k * HW, c * CW + (k + 1) * HW) for c in range(CH)] for k in range(2)]
    my_half = pl.ds(pl.multiple_of(core * HW, HW), HW)
    row8 = lax.broadcasted_iota(jnp.int32, (8, HW), 0)
    row16 = lax.broadcasted_iota(jnp.int32, (16, HW), 0)

    def cx_copy(c):
        return remote(cx.at[1 - core, c], cxr.at[c], cx_send.at[c], cx_recv.at[c], twin)

    def carry(c):
        win[:, cols(c)] = (x_ref[:, cols(c)].astype(F32) * te[:, cols(c)]).astype(BF)
        part = mm(bm, win[:, cols(c)], 0, 0)
        for k in range(2):
            cx[k, c, 0:N, :] = part[:, k * HW : (k + 1) * HW]
            gain = jnp.broadcast_to(ee[Q - 1 : Q, halves[k][c]], (8, HW))
            cx[k, c, N : N + 8, :] = jnp.where(row8 == 0, gain, keep)

    def first(a, b):
        return jnp.where(core == 0, a, b), jnp.where(core == 0, b, a)

    def gains(c):
        mine, its = cx[core, c, N : N + 8, :], cxr[c, N : N + 8, :]
        (d0, d1), (k0, k1) = first(mine[0:1], its[0:1]), first(mine[1:2], its[1:2])
        return d0, d1, k0, k1

    def message(ref, c, carry, gain):
        up = gain.astype(BF).astype(F32)
        ref[c, 0:N, :] = carry.astype(BF)
        ref[c, N : N + 16, :] = jnp.where(row16 == 0, up, jnp.where(row16 == 1, gain - up, 0.0)).astype(BF)

    def extend(ref, r, c, total):
        g = ref[r - 1, c, N : N + 16, :].astype(F32)
        return (g[0:1] + g[1:2]) * total + ref[r - 1, c, 0:N, :].astype(F32)

    def sx_copy(c):
        return remote(sx.at[c], stt.at[c, :, my_half], sx_send.at[c], sx_recv.at[c], twin)

    def f_copy(c, r):
        return remote(fb.at[c], fbr.at[r - 1, c], f_send.at[c, r - 1], f_recv.at[c, r - 1], xdev(r))

    def states_send(c):
        cx_copy(c).wait_recv()
        d0, d1, k0, k1 = gains(c)
        c0, c1 = first(cx[core, c, 0:N, :], cxr[c, 0:N, :])
        message(fb, c, d1 * k1 * c0 + c1, d1 * k1 * d0 * k0)
        for r in (1, 2, 3):

            @pl.when(x + r < 4)
            def _():
                f_copy(c, r).start()

    def states_done(c):
        sacc[c] = jnp.zeros((N, HW), F32)
        for r in (3, 2, 1):

            @pl.when(x >= r)
            def _():
                f_copy(c, r).wait_recv()
                sacc[c] = extend(fbr, r, c, sacc[c])

        d0, d1, k0, k1 = gains(c)
        c0, c1 = first(cx[core, c, 0:N, :], cxr[c, 0:N, :])
        st0 = k0 * sacc[c]
        st1 = k1 * (d0 * st0 + c0)
        mine, its = first(st0, st1)
        stt[c, :, my_half] = mine.astype(BF)
        sx[c] = its.astype(BF)
        sx_copy(c).start()

    def al_copy(c):
        return remote(al.at[c, 1 - core], alr.at[c], al_send.at[c], al_recv.at[c], twin)

    def a_copy(c, r):
        return remote(ab.at[c], abr.at[r - 1, c], a_send.at[c, r - 1], a_recv.at[c, r - 1], xdev(4 - r))

    def ax_copy(c):
        return remote(ax.at[c], adt.at[c, :, my_half], ax_send.at[c], ax_recv.at[c], twin)

    def adjoint_send(c):
        al_copy(c).wait_recv()
        d0, d1, k0, k1 = gains(c)
        a0, a1 = first(al[c, core], alr[c])
        message(ab, c, k0 * (d0 * k1 * a1 + a0), d1 * k1 * d0 * k0)
        for r in (1, 2, 3):

            @pl.when(x >= r)
            def _():
                a_copy(c, r).start()

    def adjoint_done(c):
        sacc[c] = jnp.zeros((N, HW), F32)
        for r in (3, 2, 1):

            @pl.when(x + r < 4)
            def _():
                a_copy(c, r).wait_recv()
                sacc[c] = extend(abr, r, c, sacc[c])

        d0, d1, k0, k1 = gains(c)
        a0, a1 = first(al[c, core], alr[c])
        ad1 = sacc[c]
        mine, its = first(k1 * (d1 * ad1 + a1), ad1)
        adt[c, :, my_half] = mine.astype(BF)
        ax[c] = its.astype(BF)
        ax_copy(c).start()

    scores = mm(cm, bm, 1, 1)
    ii = lax.broadcasted_iota(jnp.int32, (Q, Q), 0)
    jj = lax.broadcasted_iota(jnp.int32, (Q, Q), 1)
    causal = ii >= jj
    mlane = lax.broadcasted_iota(jnp.int32, (1, CW), 1) // PS
    masks = [jnp.where(mlane == k, 1.0, 0.0).astype(BF) for k in range(HC)]

    def intra(c):
        xc = x_ref[:, cols(c)]
        for k in range(HC):
            h = c * HC + k
            gap = colbuf[:, h : h + 1] - rowbuf[h : h + 1, :]
            w = jnp.where(causal, jnp.exp(jnp.minimum(gap, 0.0)), 0.0)
            wt[h] = w
            mix[h] = (w * scores).astype(BF)
            xm[c, k * Q : (k + 1) * Q, :] = xc * masks[k]
        acc = skip_row[:, c * CW : (c + 1) * CW] * xc.astype(F32)
        for k in range(HC):
            acc = acc + mm(mix[c * HC + k], xm[c, k * Q : (k + 1) * Q, :])
        yi[:, cols(c)] = acc

    ozsends = []

    def share_og(u):
        remote(ogs.at[pl.ds(u * RS, RS), :], oga.at[ogrows(z, u), :], oy_send.at[u], oy_recv.at[u], partner).wait_recv()
        for r in (1, 3, 2):
            piece = oga.at[ogrows(z, u), :]
            cp = remote(piece, piece, oz_send.at[r - 1, u], oz_recv.at[r - 1, u], zdev(r))
            cp.start()
            ozsends.append(cp)


    osends = []

    def output(c):
        sx_copy(c).wait_recv()
        o = yi[:, cols(c)] + ee[:, cols(c)] * mm(cm, stt[c])
        outs[c, 0:Q, :] = o.astype(BF)
        cp = remote(outs.at[c, pl.ds(0, Q), :], outs.at[c, pl.ds(Q, Q), :], o_send.at[c], o_recv.at[c], partner)
        cp.start()
        osends.append(cp)

    fsends = []
    HR = 128

    def chip(r):
        return lax.rem(x + r, 4)

    def wr_copy(c, k):
        rows = pl.ds(k * HR, HR)
        piece = wb.at[c, chip(3 if k == 0 else 1) * 2 + core, rows]
        return remote(piece, piece, wr_send.at[c, k], wr_recv.at[c, k], xdev(1 if k == 0 else 3))

    def relay_w(c):
        for k, r in ((0, 1), (1, 3)):
            w_copy(c, r).wait_recv()
            cp = wr_copy(c, k)
            cp.start()
            fsends.append(cp)
            cp = w_twin(c, 1 + k, chip(3 if k == 0 else 1) * 2 + core)
            cp.start()
            fsends.append(cp)

    def share_w(c):
        for k in range(2):
            wr_copy(c, k).wait_recv()
        cp = w_twin(c, 3, chip(2) * 2 + core)
        cp.start()
        fsends.append(cp)

    hsends = []

    def head(c):
        for j, r in enumerate((0, 3, 1, 2)):
            w_twin(c, j, chip(r) * 2 + 1 - core).wait_recv()
        wmat = wb[c].reshape(8 * 256, CW)
        hs[c] = mm(oga[Q : 2 * Q, :], wmat).astype(BF)
        cp = remote(hs.at[c], hr.at[c], h_send.at[c], h_recv.at[c], partner)
        cp.start()
        hsends.append(cp)
        hp[c] = mm(oga[0:Q, :], wmat)

    def head_grad(c):
        remote(hs.at[c], hr.at[c], h_send.at[c], h_recv.at[c], partner).wait_recv()
        g = (hp[c] + hr[c].astype(F32)).astype(BF)
        gg[:, cols(c)] = g
        wgc = (g.astype(F32) * ee[:, cols(c)]).astype(BF)
        wg[:, cols(c)] = wgc
        local = mm(cm, wgc, 0, 0)
        for k in range(2):
            al[c, k] = local[:, k * HW : (k + 1) * HW]
        al_copy(c).start()

    def within_grads(c):
        gc = gg[:, cols(c)]
        prod = mm(gc, xm[c], 1, 1)
        acc = skip_row[:, c * CW : (c + 1) * CW] * gc.astype(F32)
        tot = None
        for k in range(HC):
            h = c * HC + k
            paired = (wt[h] * prod[:, k * Q : (k + 1) * Q]).astype(BF).astype(F32)
            tot = paired if tot is None else tot + paired
            acc = acc + mm(mix[h], gc * masks[k], 0, 0)
        psum[...] = tot if c == 0 else psum[...] + tot
        gi[:, cols(c)] = acc

    def finish(c):
        ax_copy(c).wait_recv()
        gin_ref[:, cols(c)] = (gi[:, cols(c)] + te[:, cols(c)] * mm(bm, adt[c])).astype(BF)
        nb = mm(win[:, cols(c)], adt[c], 1, 1)
        nc = mm(wg[:, cols(c)], stt[c], 1, 1)
        gb_ref[...] = nb if c == 0 else gb_ref[...] + nb
        gc_ref[...] = nc if c == 0 else gc_ref[...] + nc

    dsends = []

    def dc_copy(c, r):
        return remote(ds.at[c, r], dr.at[c, r], dc_send.at[c, r], dc_recv.at[c, r], twin)

    def da_copy(c, k):
        return remote(
            da.at[c, pl.ds(k * HR, HR)], dar.at[c, k], da_send.at[c, k], da_recv.at[c, k], xdev(1 if k == 0 else 3)
        )

    def db_copy(c, k):
        return remote(db.at[c, k], dbr.at[c, k], db_send.at[c, k], db_recv.at[c, k], xdev(1 if k == 0 else 3))

    def begin(cp):
        cp.start()
        dsends.append(cp)

    def turn(k):
        ogt[k, :, Q : 2 * Q] = jnp.transpose(oga[Q : 2 * Q, pl.ds(pl.multiple_of(k * 256, 256), 256)])

    def weight_partial(c):
        remote(outs.at[c, pl.ds(0, Q), :], outs.at[c, pl.ds(Q, Q), :], o_send.at[c], o_recv.at[c], partner).wait_recv()
        oc = outs[c]
        for r in (2, 1, 3, 0):
            block = chip(r) * 2 + 1 - core
            if c == 0:
                turn(block)
            ds[c, r] = mm(ogt[block], oc).astype(BF)
            begin(dc_copy(c, r))

    def weight_send(c):
        oc = outs[c]
        for r in (2, 1, 3, 0):
            block = chip(r) * 2 + core
            if c == 0:
                turn(block)
            own = mm(ogt[block], oc)
            dc_copy(c, r).wait_recv()
            both = own + dr[c, r].astype(F32)
            if r == 0:
                gw_ref[:, cols(c)] = both
            elif r == 2:
                da[c] = both.astype(BF)
                begin(da_copy(c, 0))
                begin(da_copy(c, 1))
            else:
                dk[c, r // 2] = both

    def weight_relay(c):
        for k in range(2):
            da_copy(c, k).wait_recv()
            both, part = dk[c, k], dar[c, k].astype(F32)
            rows = slice(k * HR, (k + 1) * HR)
            rest = slice((1 - k) * HR, (2 - k) * HR)
            db[c, k, rows, :] = (both[rows] + part).astype(BF)
            db[c, k, rest, :] = both[rest].astype(BF)
            begin(db_copy(c, k))

    def weight_sum(c):
        tot = gw_ref[:, cols(c)]
        for k in range(2):
            db_copy(c, k).wait_recv()
            tot = tot + dbr[c, k].astype(F32)
        gw_ref[:, cols(c)] = tot

    for c in range(CH):
        carry(c)
    pl.semaphore_wait(bar, len(peers))
    for c in range(CH):
        cx_copy(c).start()
    for cp in ogl:
        cp.wait()
    oysends = []
    for u in range(SUB):
        cp = remote(ogs.at[pl.ds(u * RS, RS), :], oga.at[ogrows(z, u), :], oy_send.at[u], oy_recv.at[u], partner)
        cp.start()
        oysends.append(cp)
    send_w(0)
    states_send(0)
    states_send(1)
    states_send(2)
    states_send(3)
    intra(0)
    share_og(0)
    share_og(1)
    send_w(1)
    intra(1)
    states_done(0)
    relay_w(0)
    share_og(2)
    intra(2)
    states_done(1)
    send_w(2)
    output(0)
    share_og(3)
    intra(3)
    states_done(2)
    output(1)
    states_done(3)
    send_w(3)
    output(2)
    output(3)
    for cp in locs:
        cp.wait()
    for k in range(8):
        ogt[k, :, 0:Q] = jnp.transpose(oga[0:Q, k * 256 : (k + 1) * 256])
    share_w(0)
    relay_w(1)
    for r in (1, 2, 3):
        frm = lax.rem(z + 4 - r, 4)
        for u in range(SUB):
            piece = oga.at[ogrows(frm, u), :]
            remote(piece, piece, oz_send.at[r - 1, u], oz_recv.at[r - 1, u], zdev(r)).wait_recv()
    weight_partial(0)
    relay_w(2)
    head(0)
    weight_send(0)
    relay_w(3)
    share_w(1)
    weight_partial(1)
    head(1)
    weight_send(1)
    weight_relay(0)
    share_w(2)
    weight_partial(2)
    head(2)
    weight_send(2)
    weight_relay(1)
    share_w(3)
    head(3)
    weight_partial(3)
    head_grad(0)
    adjoint_send(0)
    weight_send(3)
    weight_relay(2)
    head_grad(1)
    adjoint_send(1)
    within_grads(0)
    head_grad(2)
    adjoint_done(0)
    adjoint_send(2)
    within_grads(1)
    head_grad(3)
    adjoint_send(3)
    weight_relay(3)
    adjoint_done(1)
    finish(0)
    adjoint_done(2)
    finish(1)
    within_grads(2)
    finish(2)
    adjoint_done(3)
    within_grads(3)
    finish(3)
    weight_sum(0)
    weight_sum(1)
    pb = psum[...].astype(BF)
    gb_ref[...] = gb_ref[...] + mm(pb, cm, 0, 0)
    gc_ref[...] = gc_ref[...] + mm(pb, bm)
    weight_sum(2)
    weight_sum(3)

    for cp in wsends + oysends + ozsends + fsends + osends + hsends + dsends:
        cp.wait_send()
    for c in range(CH):
        cx_copy(c).wait_send()
        sx_copy(c).wait_send()
        al_copy(c).wait_send()
        ax_copy(c).wait_send()
    for r in (1, 2, 3):

        @pl.when(x + r < 4)
        def _():
            for c in range(CH):
                f_copy(c, r).wait_send()

        @pl.when(x >= r)
        def _():
            for c in range(CH):
                a_copy(c, r).wait_send()


def hand_out(*refs):
    n = len(refs) // 3
    src, dst, held, sem = refs[:n], refs[n : 2 * n], refs[2 * n : 3 * n], refs[3 * n]
    parts = [(k, pl.ds(i * 64, 64), sem.at[:, k, i]) for k in range(n) for i in range(4)]
    ins = [pltpu.make_async_copy(src[k].at[rows], held[k].at[rows], s.at[0]) for k, rows, s in parts]
    outs = [pltpu.make_async_copy(held[k].at[rows], dst[k].at[rows], s.at[1]) for k, rows, s in parts]
    for cp in ins:
        cp.start()
    for a, b in zip(ins, outs):
        a.wait()
        b.start()
    for cp in outs:
        cp.wait()


def body(ssm_input, b_input, c_input, step_size, decay_rate, skip_gain, resets, out_grad, out_weight):
    vm, anym = pl.BlockSpec(memory_space=pltpu.VMEM), pl.BlockSpec(memory_space=pl.ANY)
    width = HEADS * PS
    dma = pltpu.SemaphoreType.DMA
    v = pltpu.VMEM
    HW = CW // 2
    scratch = [
        v((CH, 8, 256, CW), BF), v((2 * Q, 2048), BF), v((64, 2048), BF), v((8, 256, 2 * Q), BF),
        v((CH, HC * Q, CW), BF), v((HEADS, Q, Q), BF), v((HEADS, Q, Q), F32),
        v((Q, width), F32), v((Q, width), F32), v((Q, width), BF), v((Q, width), BF),
        v((CH, N, CW), BF), v((CH, N, CW), BF),
        v((Q, width), F32), v((CH, 2 * Q, CW), BF), v((CH, Q, CW), F32), v((CH, Q, CW), BF), v((CH, Q, CW), BF),
        v((Q, width), BF), v((Q, width), F32),
        v((2, CH, N + 8, HW), F32), v((CH, N + 8, HW), F32), v((CH, N + 16, HW), BF), v((3, CH, N + 16, HW), BF),
        v((CH, N, HW), F32), v((CH, N, HW), BF), v((CH, 2, N, HW), F32), v((CH, N, HW), F32),
        v((CH, N + 16, HW), BF), v((3, CH, N + 16, HW), BF), v((CH, N, HW), BF),
        v((CH, 4, 256, CW), BF), v((CH, 4, 256, CW), BF), v((CH, 256, CW), BF), v((CH, 2, 128, CW), BF),
        v((CH, 2, 256, CW), F32), v((CH, 2, 256, CW), BF), v((CH, 2, 256, CW), BF),
        v((128, Q), F32), v((Q, 128), F32), v((Q, Q), F32),
        dma((CH,)), dma((2, 8)), dma((CH, 2)), dma((CH, 2)), dma((CH, 2)), dma((CH, 2)), dma((CH, 4)), dma((CH, 4)),
        dma((SUB,)), dma((SUB,)), dma((3, SUB)), dma((3, SUB)),
        dma((CH,)), dma((CH,)), dma((CH, 3)), dma((CH, 3)), dma((CH,)), dma((CH,)),
        dma((CH,)), dma((CH,)), dma((CH, 3)), dma((CH, 3)), dma((CH,)), dma((CH,)),
        dma((CH,)), dma((CH,)), dma((CH,)), dma((CH,)), dma((CH, 4)), dma((CH, 4)),
        dma((CH, 2)), dma((CH, 2)), dma((CH, 2)), dma((CH, 2)),
    ]
    results = pl.pallas_call(
        kernel,
        out_shape=(
            jax.ShapeDtypeStruct((Q, width), BF),
            jax.ShapeDtypeStruct((Q, N), F32),
            jax.ShapeDtypeStruct((Q, N), F32),
            jax.ShapeDtypeStruct((256, width), F32),
        ),
        in_specs=[vm, vm, vm, vm, vm, vm, pl.BlockSpec(memory_space=pltpu.SMEM), anym, anym],
        out_specs=(vm, vm, vm, vm),
        scratch_shapes=scratch,
        compiler_params=pltpu.CompilerParams(
            collective_id=0, has_side_effects=True, vmem_limit_bytes=60 * 2**20
        ),
        name="block_backward",
    )(
        ssm_input[0], b_input[0], c_input[0], step_size[0], decay_rate.reshape(1, HEADS),
        skip_gain.reshape(1, HEADS), resets, out_grad[0], out_weight,
    )
    gin, gb, gc, gw = pl.pallas_call(
        hand_out,
        out_shape=[jax.ShapeDtypeStruct(a.shape, a.dtype) for a in results],
        in_specs=[anym] * 4,
        out_specs=[anym] * 4,
        scratch_shapes=[v(a.shape, a.dtype) for a in results] + [dma((2, 4, 4))],
        name="hand_out",
    )(*results)
    return gin[None], gb[None], gc[None], gw


def solution(mesh):
    in_specs = (
        P("dp", "seq", "tensor"),
        P("dp", "seq", "tensor"),
        P("dp", "seq", "tensor"),
        P("dp", "tensor", "seq"),
        P("tensor"),
        P("tensor"),
        P("dp", "seq"),
        P("dp", "seq", None),
        P(("seq", "dp"), "tensor"),
    )
    out_specs = (
        P("dp", "seq", "tensor"),
        P("dp", "seq", "tensor"),
        P("dp", "seq", "tensor"),
        P(("seq", "dp"), "tensor"),
    )
    return jax.shard_map(body, mesh=mesh, in_specs=in_specs, out_specs=out_specs, check_vma=False)
```
